32 devices in a mesh: dp: 8 (over z, y), tensor: 4 (over x, core).
Axes of the slice: x: 2, y: 2, z: 4, core: 2. Of those that a mesh axis runs over, the one named last changes fastest.
Arguments:
- layer_in: bfloat16 [16, 1024, 768], P('dp', 'tensor'), may hold values from -6 to 6
- prefix_len: int32 [16], P('dp'), may hold values from 102 to 512
- time_step: int32 [16], P('dp'), may hold values from 0 to 999
- norm_gain: bfloat16 [768], P('dp'), may hold values from 0.099609375 to 1.8984375
- qkv_weight: bfloat16 [768, 3, 768], P('dp', None, 'tensor'), may hold values from -0.21875 to 0.21875
- mix_weight: bfloat16 [768, 768], P('tensor', 'dp'), may hold values from -1.75 to 1.75
- ada_weight: bfloat16 [768, 2, 768], P('dp', None, 'tensor'), may hold values from -0.21875 to 0.21875
- up_weight: bfloat16 [768, 3072], P('dp', 'tensor'), may hold values from -0.21875 to 0.21875
- down_weight: bfloat16 [3072, 768], P('tensor', 'dp'), may hold values from -0.109375 to 0.109375
- out_grad: bfloat16 [16, 1024, 768], P('dp', 'tensor'), may hold values from -6 to 6
Outputs:
- layer_out: bfloat16 [16, 1024, 768], P('dp', 'tensor')
- in_grad: bfloat16 [16, 1024, 768], P('dp', 'tensor')
- gain_grad: float32 [768], P('dp')
- qkv_grad: float32 [768, 3, 768], P('dp', None, 'tensor')
- mix_grad: float32 [768, 768], P('tensor', 'dp')
- ada_grad: float32 [768, 2, 768], P('dp', None, 'tensor')
- up_grad: float32 [768, 3072], P('dp', 'tensor')
- down_grad: float32 [3072, 768], P('tensor', 'dp')
The draws below stay inside these ranges and needn't reach their ends.
All inputs are finite; a program needn't handle non-finite values.
Results may differ from the reference program's by a relative error of at most 0.017.
Values may be sent and summed in bfloat16 or wider, within the bound.
A program may use at most 128 MiB of HBM per device.

```python
import math
import jax
import jax.numpy as jnp
from jax import lax

HEADS = 12
HD = 64
D = 768
FF = 3072
L = 1024
B = 16


def with_ends(array, stream_key, low, top_value):
    spot = [jax.random.randint(jax.random.fold_in(stream_key, axis), (), 0, length) for axis, length in enumerate(array.shape)]
    widest = array.shape.index(max(array.shape))
    beside = spot[:widest] + [(spot[widest] + 1) % array.shape[widest]] + spot[widest + 1:]
    return array.at[tuple(spot)].set(low).at[tuple(beside)].set(top_value)


def spiked(values, own_key, source, target, blocks, factor):
    owner, partner = [(jnp.arange(values.shape[axis_at]) // (values.shape[axis_at] // blocks)).reshape([-1 if axis == axis_at else 1 for axis in range(values.ndim)]) for axis_at in (source, target)]
    chosen = jax.random.permutation(own_key, blocks)[partner]
    strong = (owner == chosen) | (owner == (partner + blocks // 2) % blocks)
    return jnp.where(strong, factor * values, values)


def block_scale(stream_key, dims, cuts, least, top_value):
    def one(axis_at, blocks):
        draws = jax.random.uniform(jax.random.fold_in(jax.random.fold_in(stream_key, 6), axis_at), (blocks,), jnp.float32, least / len(cuts), top_value / len(cuts))
        return jnp.repeat(jnp.exp(draws), dims[axis_at] // blocks).reshape((-1,) + (1,) * (len(dims) - axis_at - 1))

    level = one(*cuts[0])
    for cut in cuts[1:]:
        level = level * one(*cut)
    return level


def scatter_about(own_key, dims, spread, reach, cuts=(), kind=jnp.bfloat16):
    drawn = jax.random.normal(own_key, dims, jnp.float32) * spread
    if len(cuts) > 0:
        drawn = block_scale(own_key, dims, cuts, -0.22, 0.18) * drawn
    return jnp.clip(drawn, min=-reach, max=reach).astype(kind)


def gaussian_with(rng, shape, width, bound, shards, heavy, kind=jnp.bfloat16):
    entries = width * jax.random.normal(rng, shape, jnp.float32)
    if shards:
        entries = entries * block_scale(rng, shape, shards, -0.22, 0.18)
    return jnp.clip(spiked(entries, jax.random.fold_in(rng, 3), *heavy), -bound, bound).astype(kind)


def setup_inputs(seed: int = 0) -> dict:
    streams_of = jax.random.split(jax.random.key(seed), 11)
    return {
        "layer_in": gaussian_with(streams_of[0], (B, L, D), 1.0, 6.0, ((0, 8), (1, 4)), (0, 2, 8, 2.0)),
        "prefix_len": with_ends(jax.random.randint(streams_of[1], (B,), L // 10, L // 2 + 1), jax.random.fold_in(streams_of[1], 1), L // 10, (L // 2 + 1) - 1).astype(jnp.int32),
        "time_step": with_ends(jax.random.randint(streams_of[2], (B,), 0, 1000), jax.random.fold_in(streams_of[2], 1), 0, 999).astype(jnp.int32),
        "norm_gain": jnp.clip(1.0 + 0.18 * jax.random.normal(streams_of[3], (D,), jnp.float32), 0.099609375, 1.8984375).astype(jnp.bfloat16),
        "qkv_weight": scatter_about(streams_of[4], (D, 3, D), D ** -0.5, 0.21875, ((0, 8), (2, 4))),
        "mix_weight": scatter_about(streams_of[5], (D, D), (max(D * 16 // L, 1)) ** -0.5, 1.75, ((0, 4), (1, 8))),
        "ada_weight": scatter_about(streams_of[6], (D, 2, D), D ** -0.5, 0.21875, ((0, 8), (2, 4))),
        "up_weight": scatter_about(streams_of[7], (D, FF), D ** -0.5, 0.21875, ((0, 8), (1, 4))),
        "down_weight": scatter_about(streams_of[8], (FF, D), FF ** -0.5, 0.109375, ((0, 4), (1, 8))),
        "out_grad": gaussian_with(streams_of[9], (B, L, D), 1.0, 6.0, ((0, 8), (1, 4)), (0, 2, 8, 2.0)),
    }


@jax.custom_vjp
def low(v):
    return lax.optimization_barrier(v.astype(jnp.bfloat16)).astype(jnp.float32)

@jax.custom_vjp
def low_back(v):
    return v

def low_keep(v):
    return (low(v), None)

def low_pass(kept, grad):
    return (grad,)

def back_keep(v):
    return (v, None)

def back_low(kept, grad):
    return (low(grad),)
low.defvjp(low_keep, low_pass)
low_back.defvjp(back_keep, back_low)
EPS = 1e-05
HIGH = lax.Precision.HIGHEST

def normalize(values):
    mean_val = lax.optimization_barrier(jnp.mean(values, axis=-1, keepdims=True))
    centred = values - mean_val
    return centred * lax.rsqrt(lax.optimization_barrier(jnp.mean(centred * centred, axis=-1, keepdims=True)) + EPS)

def gelu_tanh(values):
    return 0.5 * values * (1.0 + jnp.tanh(0.7978845608028654 * (values + 0.044715 * values * values * values)))

def time_features(time_step, feat_width):
    half_width = feat_width // 2
    inv_freq = jnp.exp(jnp.arange(half_width, dtype=jnp.float32) * (-math.log(10000.0) / half_width))
    angles = time_step.astype(jnp.float32)[:, None] * inv_freq[None, :]
    return jnp.concatenate([jnp.sin(angles), jnp.cos(angles)], axis=1)

def rotary_tables(length, head_size):
    half_size = head_size // 2
    inv_freq = jnp.exp(jnp.arange(half_size, dtype=jnp.float32) * (-math.log(10000.0) / half_size))
    angles = jnp.arange(length, dtype=jnp.float32)[:, None] * inv_freq[None, :]
    return (jnp.cos(angles)[:, None, :], jnp.sin(angles)[:, None, :])

def rotate(values, cosine, sine_tab):
    half_size = values.shape[-1] // 2
    first_half = values[..., :half_size]
    second = values[..., half_size:]
    return jnp.concatenate([first_half * cosine - second * sine_tab, second * cosine + first_half * sine_tab], axis=-1)

def allowed_mask(row_start, block_rows, length, prefix_one):
    row_pos = row_start + jnp.arange(block_rows, dtype=jnp.int32)
    key_pos = jnp.arange(length, dtype=jnp.int32)
    return (key_pos[None, :] <= row_pos[:, None]) | (key_pos[None, :] < prefix_one)

def layer(layer_x, weight_set, prefix_one, emb_one):
    gain_f, qkv_f, mix_f, ada_f, up_f, down_f = weight_set
    length = layer_x.shape[0]
    normed1 = normalize(layer_x)
    attn_in = low(normed1 * gain_f)
    qkv_all = jnp.einsum('ld,dch->lch', attn_in, qkv_f, precision=HIGH)
    cosine, sine_tab = rotary_tables(length, HD)
    q_rot = low(rotate(low_back(qkv_all[:, 0].reshape(length, HEADS, HD)), cosine, sine_tab))
    k_rot = low(rotate(low_back(qkv_all[:, 1].reshape(length, HEADS, HD)), cosine, sine_tab))
    v_heads = low(low_back(qkv_all[:, 2].reshape(length, HEADS, HD)))
    scores = low_back(jnp.einsum('qhd,khd->hqk', q_rot, k_rot, precision=HIGH) * (1.0 / math.sqrt(HD)))
    mask_all = allowed_mask(0, length, length, prefix_one)
    scores = jnp.where(mask_all[None], scores, -1e+30)
    row_max = lax.optimization_barrier(jnp.max(scores, axis=-1, keepdims=True))
    exp_scores = jnp.exp(scores - row_max)
    attn_prob = low(exp_scores / lax.optimization_barrier(jnp.sum(exp_scores, axis=-1, keepdims=True)))
    attn_mix = jnp.einsum('hqk,khd->qhd', attn_prob, v_heads, precision=HIGH).reshape(length, HEADS * HD)
    attn_mix = low(low_back(attn_mix))
    resid = layer_x + low_back(jnp.dot(attn_mix, mix_f, precision=HIGH))
    normed2 = normalize(resid)
    ada_vec = jnp.einsum('d,dch->ch', emb_one, ada_f, precision=HIGH)
    mlp_in = low(normed2 * (1.0 + ada_vec[0]) + ada_vec[1])
    gate_pre = low_back(jnp.dot(mlp_in, up_f, precision=HIGH))
    hidden = low(gelu_tanh(gate_pre))
    return resid + low_back(jnp.dot(hidden, down_f, precision=HIGH))

def reference(layer_in, prefix_len, time_step, norm_gain, qkv_weight, mix_weight, ada_weight, up_weight, down_weight, out_grad):
    weights = tuple((weight_item.astype(jnp.float32) for weight_item in (norm_gain, qkv_weight, mix_weight, ada_weight, up_weight, down_weight)))
    time_emb = low(time_features(time_step, D))
    zero_grads = tuple((jnp.zeros(weight_item.shape, jnp.float32) for weight_item in weights))

    def per_sequence(totals, inputs_one):
        seq_in, prefix_one, emb_one, grad_one = inputs_one

        def forward_fn(layer_x, *weight_set):
            return layer(layer_x, weight_set, prefix_one, emb_one)
        seq_out, back_fn = jax.vjp(forward_fn, seq_in.astype(jnp.float32), *weights)
        grad_set = back_fn(grad_one.astype(jnp.float32))
        totals = jax.tree.map(jnp.add, totals, tuple(grad_set[1:]))
        return (totals, (seq_out.astype(jnp.bfloat16), grad_set[0].astype(jnp.bfloat16)))
    totals, outs_pair = lax.scan(per_sequence, zero_grads, (layer_in, prefix_len, time_emb, out_grad))
    return (outs_pair[0], outs_pair[1], totals[0], totals[1], totals[2], totals[3], totals[4], totals[5])
```

```python
import functools
import math

import jax
import jax.numpy as jnp
import numpy as np
from jax import lax
from jax.experimental import pallas as pl
from jax.experimental.pallas import tpu as pltpu
from jax.sharding import PartitionSpec as P

HD = 64


EPS = 1e-05


def cut_along(shard, dim, size):
    dims = shard.shape
    parts = shard.reshape(*dims[:dim], size, dims[dim] // size, *dims[dim + 1 :])
    return jnp.moveaxis(parts, dim, 0)


def sum_at_owner(shard, axis, dim):
    size = lax.axis_size(axis)
    parts = lax.all_to_all(cut_along(shard, dim, size), axis, 0, 0, tiled=True)
    return jnp.sum(parts.astype(jnp.float32), axis=0)


def side_by_side(arrays, axis, dim, along):
    widths = [math.prod(a.shape[along:]) for a in arrays]
    both = jnp.concatenate(
        [a.reshape(*a.shape[:along], w) for a, w in zip(arrays, widths)], axis=along
    )
    filled = sum_at_owner(both, axis, dim)
    parts = jnp.split(filled, [sum(widths[:k]) for k in range(1, len(widths))], axis=along)
    return tuple(
        (b.reshape(*filled.shape[:along], *a.shape[along:]) for a, b in zip(arrays, parts))
    )


def sent_together(arrays, axis, dim, along):
    widths = [a.shape[along] for a in arrays]
    both = jnp.concatenate(arrays, axis=along)
    filled = sum_at_owner(both, axis, dim)
    return tuple(jnp.split(filled, [sum(widths[:k]) for k in range(1, len(widths))], axis=along))


def normalize(values):
    mean_val = jnp.mean(values, axis=-1, keepdims=True)
    centred = values - mean_val
    inv_std = lax.rsqrt(jnp.mean(centred * centred, axis=-1, keepdims=True) + EPS)
    return (centred * inv_std, inv_std)


def norm_back(grad_norm, normed, inv_std):
    mean_grad = jnp.mean(grad_norm, axis=-1, keepdims=True)
    mean_cross = jnp.mean(grad_norm * normed, axis=-1, keepdims=True)
    return inv_std * (grad_norm - mean_grad - normed * mean_cross)


def gelu_tanh(values):
    return (
        0.5
        * values
        * (1.0 + jnp.tanh(0.7978845608028654 * (values + 0.044715 * values * values * values)))
    )


def time_features(time_step, feat_width):
    half_width = feat_width // 2
    inv_freq = jnp.exp(
        jnp.arange(half_width, dtype=jnp.float32) * (-math.log(10000.0) / half_width)
    )
    angles = time_step.astype(jnp.float32)[:, None] * inv_freq[None, :]
    return jnp.concatenate([jnp.sin(angles), jnp.cos(angles)], axis=1)


def rotary_tables(length, head_size):
    half_size = head_size // 2
    inv_freq = jnp.exp(jnp.arange(half_size, dtype=jnp.float32) * (-math.log(10000.0) / half_size))
    angles = jnp.arange(length, dtype=jnp.float32)[:, None] * inv_freq[None, :]
    return (jnp.cos(angles)[:, None, :], jnp.sin(angles)[:, None, :])


def rotate(values, cosine, sine_tab):
    half_size = values.shape[-1] // 2
    first_half = values[..., :half_size]
    second = values[..., half_size:]
    return jnp.concatenate(
        [first_half * cosine - second * sine_tab, second * cosine + first_half * sine_tab], axis=-1
    )


def unrotate(grad_rot, cosine, sine_tab):
    half_size = grad_rot.shape[-1] // 2
    first_half = grad_rot[..., :half_size]
    second = grad_rot[..., half_size:]
    return jnp.concatenate(
        [first_half * cosine + second * sine_tab, second * cosine - first_half * sine_tab], axis=-1
    )


def allowed_mask(row_start, block_rows, length, prefix_one):
    row_pos = row_start + jnp.arange(block_rows, dtype=jnp.int32)
    key_pos = jnp.arange(length, dtype=jnp.int32)
    return (key_pos[None, :] <= row_pos[:, None]) | (key_pos[None, :] < prefix_one)


def block_scores(q_blk, k_rot, row_start, prefix_one):
    block_rows = q_blk.shape[0]
    score_scale = 1.0 / math.sqrt(q_blk.shape[2])
    scores = (
        jnp.einsum("qhd,khd->hqk", q_blk, k_rot, preferred_element_type=jnp.float32) * score_scale
    )
    mask_blk = allowed_mask(row_start, block_rows, k_rot.shape[0], prefix_one)
    return jnp.where(mask_blk[None], scores, -1e30)


def attend_forward(q_rot, k_rot, v_heads, prefix_one, block_rows):
    length, num_heads, head_size = q_rot.shape
    block_count = length // block_rows
    q_blocks = q_rot.reshape(block_count, block_rows, num_heads, head_size)
    starts = jnp.arange(block_count, dtype=jnp.int32) * block_rows

    def one_block(block_in):
        q_blk, row_start = block_in
        scores = block_scores(q_blk, k_rot, row_start, prefix_one)
        row_max = jnp.max(scores, axis=-1, keepdims=True)
        exp_scores = jnp.exp(scores - row_max)
        exp_total = jnp.sum(exp_scores, axis=-1, keepdims=True)
        attn_prob = (exp_scores / exp_total).astype(jnp.bfloat16)
        attn_mix = jnp.einsum(
            "hqk,khd->qhd", attn_prob, v_heads, preferred_element_type=jnp.float32
        )
        return (attn_mix, (row_max + jnp.log(exp_total))[..., 0])

    attn_mix, log_sum = lax.map(one_block, (q_blocks, starts))
    return (attn_mix.reshape(length, num_heads, head_size), log_sum)


def attend_backward(q_rot, k_rot, v_heads, grad_mix, log_sum, prefix_one, block_rows):
    length, num_heads, head_size = q_rot.shape
    block_count = length // block_rows
    score_scale = 1.0 / math.sqrt(head_size)
    q_blocks = q_rot.reshape(block_count, block_rows, num_heads, head_size)
    g_blocks = grad_mix.reshape(block_count, block_rows, num_heads, head_size)
    starts = jnp.arange(block_count, dtype=jnp.int32) * block_rows

    def one_block(grad_carry, block_in):
        grad_k, grad_v = grad_carry
        q_blk, g_blk, lse_blk, row_start = block_in
        scores = block_scores(q_blk, k_rot, row_start, prefix_one)
        attn_soft = jnp.exp(scores - lse_blk[..., None])
        attn_prob = attn_soft.astype(jnp.bfloat16)
        grad_p = jnp.einsum("qhd,khd->hqk", g_blk, v_heads, preferred_element_type=jnp.float32)
        row_delta = jnp.sum(grad_p * attn_soft, axis=-1, keepdims=True)
        grad_s = (attn_soft * (grad_p - row_delta)).astype(jnp.bfloat16)
        grad_q = (
            jnp.einsum("hqk,khd->qhd", grad_s, k_rot, preferred_element_type=jnp.float32)
            * score_scale
        )
        grad_k = (
            grad_k
            + jnp.einsum("hqk,qhd->khd", grad_s, q_blk, preferred_element_type=jnp.float32)
            * score_scale
        )
        grad_v = grad_v + jnp.einsum(
            "hqk,qhd->khd", attn_prob, g_blk, preferred_element_type=jnp.float32
        )
        return ((grad_k, grad_v), grad_q)

    zero_kv = jnp.zeros((length, num_heads, head_size), jnp.float32)
    carried, grad_q = lax.scan(one_block, (zero_kv, zero_kv), (q_blocks, g_blocks, log_sum, starts))
    return (grad_q.reshape(length, num_heads, head_size), carried[0], carried[1])


def seq_gather(piece):
    return lax.all_gather(piece, "tensor", axis=0, tiled=True)


def seq_sum(partial_rows):
    return lax.psum_scatter(
        partial_rows.astype(jnp.bfloat16), "tensor", scatter_dimension=0, tiled=True
    ).astype(jnp.float32)


def fetch_weights(norm_gain, qkv_weight, ada_weight, up_weight, mix_weight, down_weight):
    row_parts = (
        lax.all_gather(norm_gain, "dp", axis=0, tiled=True),
        lax.all_gather(qkv_weight, "dp", axis=0, tiled=True),
        lax.all_gather(ada_weight, "dp", axis=0, tiled=True),
        lax.all_gather(up_weight, "dp", axis=0, tiled=True),
    )
    col_parts = (
        lax.all_gather(mix_weight, "dp", axis=1, tiled=True),
        lax.all_gather(down_weight, "dp", axis=1, tiled=True),
    )
    return tuple(row_parts) + tuple(col_parts)


def reduce_owned(row_terms, col_terms):
    row_owned = side_by_side(
        (
            row_terms[0].astype(jnp.bfloat16),
            row_terms[1].astype(jnp.bfloat16),
            row_terms[2].astype(jnp.bfloat16),
            row_terms[3].astype(jnp.bfloat16),
        ),
        "dp",
        0,
        1,
    )
    col_owned = sent_together(
        (col_terms[0].astype(jnp.bfloat16), col_terms[1].astype(jnp.bfloat16)), "dp", 1, 0
    )
    return (tuple(row_owned), tuple(col_owned))


def add_tree(first_sum, second_sum):
    if first_sum is None:
        return second_sum
    return jax.tree.map(jnp.add, first_sum, second_sum)


def local(
    layer_in,
    prefix_len,
    time_step,
    norm_gain,
    qkv_weight,
    mix_weight,
    ada_weight,
    up_weight,
    down_weight,
    out_grad,
):
    micro_count, piece_len, model_width = layer_in.shape
    length = piece_len * lax.axis_size("tensor")
    block_rows = min(512, length)
    tensor_idx = lax.axis_index("tensor")
    col_width = ada_weight.shape[2]
    time_emb = time_features(time_step, model_width).astype(jnp.bfloat16)
    cosine, sine_tab = rotary_tables(length, HD)
    owned = None
    outputs = []
    in_grads = []
    for micro_idx in range(micro_count):
        current = fetch_weights(
            norm_gain, qkv_weight, ada_weight, up_weight, mix_weight, down_weight
        )
        gain_full, wq_full, wada_full, wup_full, wmix_full, wdown_full = current
        gain_f = gain_full.astype(jnp.float32)
        x_piece = layer_in[micro_idx].astype(jnp.float32)
        prefix_one = prefix_len[micro_idx]
        normed1, inv1 = normalize(x_piece)
        attn_in = seq_gather((normed1 * gain_f).astype(jnp.bfloat16))
        qkv_all = jnp.einsum("ld,dch->lch", attn_in, wq_full, preferred_element_type=jnp.float32)
        num_heads = qkv_all.shape[2] // HD
        q_rot = rotate(qkv_all[:, 0].reshape(length, num_heads, HD), cosine, sine_tab).astype(
            jnp.bfloat16
        )
        k_rot = rotate(qkv_all[:, 1].reshape(length, num_heads, HD), cosine, sine_tab).astype(
            jnp.bfloat16
        )
        v_heads = qkv_all[:, 2].reshape(length, num_heads, HD).astype(jnp.bfloat16)
        attn_mix, log_sum = attend_forward(q_rot, k_rot, v_heads, prefix_one, block_rows)
        mix_low = attn_mix.reshape(length, num_heads * HD).astype(jnp.bfloat16)
        resid = x_piece + seq_sum(jnp.dot(mix_low, wmix_full, preferred_element_type=jnp.float32))
        normed2, inv2 = normalize(resid)
        ada_cols = jnp.einsum(
            "d,dch->ch", time_emb[micro_idx], wada_full, preferred_element_type=jnp.float32
        )
        ada_all = lax.all_gather(ada_cols, "tensor", axis=1, tiled=True)
        mlp_rows = (normed2 * (1.0 + ada_all[0]) + ada_all[1]).astype(jnp.bfloat16)
        mlp_in = seq_gather(mlp_rows)
        gate_pre = jnp.dot(mlp_in, wup_full, preferred_element_type=jnp.float32)
        hidden_low = gelu_tanh(gate_pre).astype(jnp.bfloat16)
        mlp_piece = seq_sum(jnp.dot(hidden_low, wdown_full, preferred_element_type=jnp.float32))
        outputs.append((resid + mlp_piece).astype(jnp.bfloat16))
        current = fetch_weights(
            norm_gain, qkv_weight, ada_weight, up_weight, mix_weight, down_weight
        )
        gain_full, wq_full, wada_full, wup_full, wmix_full, wdown_full = current
        grad_top = out_grad[micro_idx].astype(jnp.float32)
        gelu_out, gelu_back = jax.vjp(gelu_tanh, gate_pre)
        grad_mlp = seq_gather(out_grad[micro_idx])
        grad_hidden = jnp.einsum(
            "ld,fd->lf", grad_mlp, wdown_full, preferred_element_type=jnp.float32
        )
        down_term = jnp.einsum(
            "lf,ld->fd", hidden_low, grad_mlp, preferred_element_type=jnp.float32
        )
        grad_gate = gelu_back(grad_hidden)[0].astype(jnp.bfloat16)
        up_term = jnp.einsum("ld,lf->df", mlp_in, grad_gate, preferred_element_type=jnp.float32)
        grad_u = seq_sum(
            jnp.einsum("lf,df->ld", grad_gate, wup_full, preferred_element_type=jnp.float32)
        )
        ada_term = jnp.stack([jnp.sum(grad_u * normed2, axis=0), jnp.sum(grad_u, axis=0)])
        grad_res = grad_top + norm_back(grad_u * (1.0 + ada_all[0]), normed2, inv2)
        grad_attn = seq_gather(grad_res.astype(jnp.bfloat16))
        grad_mix = jnp.einsum(
            "ld,hd->lh", grad_attn, wmix_full, preferred_element_type=jnp.float32
        ).astype(jnp.bfloat16)
        mix_term = jnp.einsum("lh,ld->hd", mix_low, grad_attn, preferred_element_type=jnp.float32)
        grad_q, grad_k, grad_v = attend_backward(
            q_rot,
            k_rot,
            v_heads,
            grad_mix.reshape(length, num_heads, HD),
            log_sum,
            prefix_one,
            block_rows,
        )
        grad_qkv = jnp.stack(
            [
                unrotate(grad_q, cosine, sine_tab).reshape(length, num_heads * HD),
                unrotate(grad_k, cosine, sine_tab).reshape(length, num_heads * HD),
                grad_v.reshape(length, num_heads * HD),
            ],
            axis=1,
        ).astype(jnp.bfloat16)
        qkv_term = jnp.einsum("ld,lch->dch", attn_in, grad_qkv, preferred_element_type=jnp.float32)
        grad_a = seq_sum(
            jnp.einsum("lch,dch->ld", grad_qkv, wq_full, preferred_element_type=jnp.float32)
        )
        gain_part = jnp.sum(grad_a * normed1, axis=0)
        ada_sum, gain_sum = lax.psum((ada_term, gain_part), "tensor")
        ada_slice = lax.dynamic_slice_in_dim(ada_sum, tensor_idx * col_width, col_width, 1)
        ada_w_term = time_emb[micro_idx].astype(jnp.float32)[:, None, None] * ada_slice[None]
        in_grads.append((grad_res + norm_back(grad_a * gain_f, normed1, inv1)).astype(jnp.bfloat16))
        row_terms = (gain_sum, qkv_term, ada_w_term, up_term)
        col_terms = (mix_term, down_term)
        owned = add_tree(owned, reduce_owned(row_terms, col_terms))
    row_owned, col_owned = owned
    return (
        jnp.stack(outputs),
        jnp.stack(in_grads),
        row_owned[0],
        row_owned[1],
        col_owned[0],
        row_owned[2],
        row_owned[3],
        col_owned[1],
    )


MESH_ID = pl.DeviceIdType.MESH
BF = jnp.bfloat16
F32 = jnp.float32
NEG = -1e30


def mm(a, b):
    return lax.dot_general(a, b, (((1,), (0,)), ((), ())), preferred_element_type=F32)


def mm_nt(a, b):
    return lax.dot_general(a, b, (((1,), (1,)), ((), ())), preferred_element_type=F32)


def mm_tn(a, b):
    return lax.dot_general(a, b, (((0,), (0,)), ((), ())), preferred_element_type=F32)


def lanes(shape):
    return lax.broadcasted_iota(jnp.int32, shape, len(shape) - 1)


def row_stats(x):
    mean = jnp.mean(x, axis=-1, keepdims=True)
    cen = x - mean
    inv = lax.rsqrt(jnp.mean(cen * cen, axis=-1, keepdims=True) + EPS)
    return mean, cen, inv


def swap_halves(x):
    low = lax.rem(lanes(x.shape), HD) < HD // 2
    return jnp.where(low, pltpu.roll(x, 128 - HD // 2, 1), pltpu.roll(x, HD // 2, 1))


def layer_kernel(
    dims,
    pref,
    small,
    xin,
    dyin,
    wsl,
    adaw,
    cos_t,
    sin_t,
    lo_out,
    ig_out,
    gw_out,
    ga_out,
    gg_out,
    W,
    X,
    DYF,
    AIN,
    MG,
    Q,
    K,
    V,
    EA,
    EB,
    EC,
    O,
    RINV,
    MT,
    RES,
    ST,
    OWN,
    PS,
    PR,
    HID,
    GP,
    M3,
    DEL,
    GQ,
    G,
    R1A,
    R1B,
    R2X,
    R2Y,
    R3,
    LOS,
    IGS,
    SMR,
    ADP,
    ADL,
    ADS,
    ADT,
    VEC,
    ACC,
    SLT,
    RTT,
    GA2,
    GAL,
    GGT,
    GGS,
    GGR,
    sx,
    sagz,
    sagx,
    sagy,
    sagdx,
    sagdy,
    sr1a,
    sr1b,
    sr2x,
    sr2y,
    sr3,
    score,
    ssm,
    sad,
    sadt,
    srt,
    sgal,
    sgt,
    sgr,
    sloc,
):
    NDP, NZ, SR, D, T, PC = dims
    HA = (2 * SR) // 3
    d = lax.axis_index("dp")
    t = lax.axis_index("tensor")
    z, y = lax.div(d, 2), lax.rem(d, 2)
    p, c = lax.div(t, 2), lax.rem(t, 2)
    px, yx, cx = 1 - p, 1 - y, 1 - c
    DX, DY_, DC = (d, px * 2 + c), (z * 2 + yx, t), (d, p * 2 + cx)

    def zi(dz):
        return lax.rem(z + dz, NZ)

    def dpeer(k):
        return lax.rem(d + k, NDP)

    def tpeer(k):
        return lax.rem(t + k, 4)

    def rc(src, dst, s, r, dev):
        return pltpu.make_async_remote_copy(
            src_ref=src, dst_ref=dst, send_sem=s, recv_sem=r, device_id=dev, device_id_type=MESH_ID
        )

    bar = pltpu.get_barrier_semaphore()
    for k in range(1, NDP):
        pl.semaphore_signal(bar, 1, device_id=(dpeer(k), t), device_id_type=MESH_ID)
    for k in range(1, 4):
        pl.semaphore_signal(bar, 1, device_id=(d, tpeer(k)), device_id_type=MESH_ID)
    pl.semaphore_wait(bar, NDP - 1 + 3)

    def cp_x():
        return rc(xin.at[px], X.at[p], sx.at[0, 0], sx.at[0, 1], DX)

    def cp_x_recv():
        return rc(xin.at[px], X.at[px], sx.at[0, 0], sx.at[0, 1], DX)

    def rows_of(j, cc):
        return pl.ds(pl.multiple_of((2 * j + cc) * PC, PC), PC)

    def cp_dy():
        return rc(dyin.at[px], DYF.at[rows_of(p, c)], sx.at[1, 0], sx.at[1, 1], DX)

    def cp_dy_recv():
        return rc(dyin.at[px], DYF.at[rows_of(px, c)], sx.at[1, 0], sx.at[1, 1], DX)

    def cp_lo():
        return rc(LOS, lo_out.at[p], sx.at[2, 0], sx.at[2, 1], DX)

    def cp_lo_recv():
        return rc(LOS, lo_out.at[px], sx.at[2, 0], sx.at[2, 1], DX)

    def cp_ig():
        return rc(IGS, ig_out.at[p], sx.at[3, 0], sx.at[3, 1], DX)

    def cp_ig_recv():
        return rc(IGS, ig_out.at[px], sx.at[3, 0], sx.at[3, 1], DX)

    def cp_full(buf, n, j):
        return rc(buf.at[rows_of(j, c)], buf.at[rows_of(j, c)], score.at[0, n, j], score.at[1, n, j], DC)

    def cp_full_recv(buf, n, j):
        return rc(buf.at[rows_of(j, cx)], buf.at[rows_of(j, cx)], score.at[0, n, j], score.at[1, n, j], DC)

    def cp_part(n, j):
        s = n % 2
        return rc(PS.at[s, j], PR.at[s, j], score.at[0, 4 + n, j], score.at[1, 4 + n, j], DC)

    def ag_z(k, dz):
        return rc(wsl.at[k], W.at[k, p, d], sagz.at[0, k, dz], sagz.at[1, k, z], (zi(dz) * 2 + y, t))

    def ag_z_recv(k, zq):
        return rc(wsl.at[k], W.at[k, p, zq * 2 + y], sagz.at[0, k, 0], sagz.at[1, k, zq], DX)

    def ag_x(k, zq, own):
        src = wsl.at[k] if own else W.at[k, p, zq * 2 + y]
        return rc(src, W.at[k, p, zq * 2 + y], sagx.at[0, k, zq], sagx.at[1, k, zq], DX)

    def ag_x_recv(k, zq):
        return rc(wsl.at[k], W.at[k, px, zq * 2 + y], sagx.at[0, k, zq], sagx.at[1, k, zq], DX)

    def ag_y(k, zq, own):
        src = wsl.at[k] if own else W.at[k, p, zq * 2 + y]
        return rc(src, W.at[k, p, zq * 2 + y], sagy.at[0, k, zq], sagy.at[1, k, zq], DY_)

    def ag_y_recv(k, zq):
        return rc(wsl.at[k], W.at[k, p, zq * 2 + yx], sagy.at[0, k, zq], sagy.at[1, k, zq], DY_)

    A_, B_ = pl.ds(0, HA), pl.ds(HA, SR - HA)

    def ag_dy(k, zq):
        r = W.at[k, px, zq * 2 + y, A_]
        return rc(r, r, sagdy.at[0, k, zq], sagdy.at[1, k, zq], DY_)

    def ag_dy_recv(k, zq):
        r = W.at[k, px, zq * 2 + yx, A_]
        return rc(r, r, sagdy.at[0, k, zq], sagdy.at[1, k, zq], DY_)

    def ag_dx(k, zq):
        r = W.at[k, p, zq * 2 + yx, B_]
        return rc(r, r, sagdx.at[0, k, zq], sagdx.at[1, k, zq], DX)

    def ag_dx_recv(k, zq):
        r = W.at[k, px, zq * 2 + yx, B_]
        return rc(r, r, sagdx.at[0, k, zq], sagdx.at[1, k, zq], DX)

    def ag_events(k):
        def first():
            ag_x(k, z, True).start()
            ag_y(k, z, True).start()

        def relay(dz):
            def run():
                zq = zi(dz)
                ag_z_recv(k, zq).wait_recv()
                ag_x(k, zq, False).start()
                ag_y(k, zq, False).start()

            return run

        def diag(dz):
            def run():
                zq = zi(dz)
                ag_x_recv(k, zq).wait_recv()
                ag_dy(k, zq).start()
                ag_y_recv(k, zq).wait_recv()
                ag_dx(k, zq).start()

            return run

        return [first, relay(1), relay(3), diag(0), relay(2), diag(1), diag(3), diag(2)]

    def ag_done(k):
        for zq in range(NZ):
            ag_dx_recv(k, zq).wait_recv()
            ag_dy_recv(k, zq).wait_recv()

    def ag_sent(k):
        for dz in range(1, NZ):
            ag_z(k, dz).wait_send()
        for zq in range(NZ):
            ag_x(k, zq, True).wait_send()
            ag_y(k, zq, True).wait_send()
            ag_dx(k, zq).wait_send()
            ag_dy(k, zq).wait_send()

    def gr(k):
        return W.at[2] if k == 0 else G.at[k - 1]

    def r1a(k, zq):
        return rc(gr(k).at[px, zq * 2 + yx, A_], R1A.at[zq], sr1a.at[0, k, zq], sr1a.at[1, k, zq], DY_)

    def r1b(k, zq):
        return rc(gr(k).at[px, zq * 2 + yx, B_], R1B.at[zq], sr1b.at[0, k, zq], sr1b.at[1, k, zq], DX)

    def r2x(k, zq):
        return rc(gr(k).at[px, zq * 2 + y], R2X.at[zq], sr2x.at[0, k, zq], sr2x.at[1, k, zq], DX)

    def r2y(k, zq):
        return rc(gr(k).at[p, zq * 2 + yx], R2Y.at[zq], sr2y.at[0, k, zq], sr2y.at[1, k, zq], DY_)

    def r3(k, dz):
        return rc(
            gr(k).at[p, zi(dz) * 2 + y], R3.at[k, z], sr3.at[0, k, dz], sr3.at[1, k, z], (zi(dz) * 2 + y, t)
        )

    def r3_recv(k, zq):
        return rc(gr(k).at[p, zq * 2 + y], R3.at[k, zq], sr3.at[0, k, 0], sr3.at[1, k, zq], DX)

    ZORD = (1, 3, 2, 0)

    def rs_start(k):
        for dz in ZORD:
            r1a(k, zi(dz)).start()
            r1b(k, zi(dz)).start()

    def rs_mid(k, dz):
        zq = zi(dz)
        g = gr(k)
        r1a(k, zq).wait_recv()
        r1b(k, zq).wait_recv()
        ia, ib = zq * 2 + y, zq * 2 + yx
        g[px, ia, A_] = (g[px, ia, A_].astype(F32) + R1A[zq].astype(F32)).astype(BF)
        g[p, ib, B_] = (g[p, ib, B_].astype(F32) + R1B[zq].astype(F32)).astype(BF)
        r2x(k, zq).start()
        r2y(k, zq).start()

    def rs_quad(k, dz):
        zq = zi(dz)
        g = gr(k)
        r2x(k, zq).wait_recv()
        r2y(k, zq).wait_recv()
        i = zq * 2 + y
        g[p, i] = (g[p, i].astype(F32) + R2X[zq].astype(F32) + R2Y[zq].astype(F32)).astype(BF)
        if dz != 0:
            r3(k, dz).start()

    def rs_final(k):
        for dz in (1, 3, 2):
            r3_recv(k, zi(dz)).wait_recv()
        g = gr(k)
        tot = g[p, d].astype(F32)
        for dz in (1, 2, 3):
            tot = tot + R3[k, zi(dz)].astype(F32)
        gw_out[k] = tot

    def rs_sent(k):
        for zq in range(NZ):
            r1a(k, zq).wait_send()
            r1b(k, zq).wait_send()
            r2x(k, zq).wait_send()
            r2y(k, zq).wait_send()
        for dz in range(1, NZ):
            r3(k, dz).wait_send()

    def rs_events(k):
        evs = [lambda: rs_start(k)]
        for dz in ZORD:
            evs.append(functools.partial(rs_mid, k, dz))
        for dz in ZORD:
            evs.append(functools.partial(rs_quad, k, dz))
        evs.append(lambda: rs_final(k))
        return evs

    def loop(n, body, events=()):
        events = dict(events)

        def step(i, carry):
            for at, fns in events.items():
                def fire(fns=fns):
                    for fn in fns:
                        fn()

                pl.when(i == at)(fire)
            body(i)
            return carry

        lax.fori_loop(0, n, step, 0)

    def sm(k):
        return rc(small.at[dpeer(k)], SMR.at[d], ssm.at[0, k], ssm.at[1, d], (dpeer(k), t))

    def sm_recv(k):
        return rc(small.at[0], SMR.at[dpeer(k)], ssm.at[0, k], ssm.at[1, dpeer(k)], DX)

    def ad(k):
        return rc(ADL.at[dpeer(k)], ADP.at[d], sad.at[0, k], sad.at[1, d], (dpeer(k), t))

    def ad_recv(k):
        return rc(ADL.at[0], ADP.at[dpeer(k)], sad.at[0, k], sad.at[1, dpeer(k)], DX)

    def adt(k):
        return rc(ADS, ADT.at[t], sadt.at[0, k], sadt.at[1, t], (d, tpeer(k)))

    def adt_recv(k):
        return rc(ADS, ADT.at[tpeer(k)], sadt.at[0, k], sadt.at[1, tpeer(k)], DX)

    own_x = pltpu.make_async_copy(xin.at[p], X.at[p], sloc.at[0])
    own_x.start()
    own_dy = pltpu.make_async_copy(dyin.at[p], DYF.at[rows_of(p, c)], sloc.at[1])
    own_dy.start()
    for k in range(1, NDP):
        sm(k).start()
    ag_ev0 = ag_events(0)
    for dz in (1, 3, 2):
        ag_z(0, dz).start()
    ag_ev0[0]()
    cp_x().start()
    for k in (1, 2):
        for dz in (1, 3, 2):
            ag_z(k, dz).start()

    SMR[d] = small[d]
    for k in range(3):
        W[k, p, d] = wsl[k]
    O[...] = jnp.zeros_like(O)
    GQ[...] = jnp.zeros_like(GQ)
    ACC[...] = jnp.zeros_like(ACC)
    SLT[...] = jnp.zeros_like(SLT)
    GA2[...] = jnp.zeros_like(GA2)
    GGS[...] = jnp.zeros_like(GGS)

    for k in range(1, NDP):
        sm_recv(k).wait_recv()
    for i in range(NDP):
        VEC[0:1, SR * i : SR * (i + 1)] = SMR[i, 2:3, 0:SR]

    feats = SMR[...].reshape(NDP * 8, 128).astype(BF)
    part = mm(feats, adaw[...])
    ADL[...] = part.reshape(NDP, 8, part.shape[1])
    for k in range(1, NDP):
        ad(k).start()
    ADP[d] = ADL[d]

    RT = 64

    def ln1(j, jj):
        def body(i):
            r = pl.ds(pl.multiple_of(i * RT, RT), RT)
            mean, cen, inv = row_stats(X[j, r, :].astype(F32))
            AIN[pl.ds(pl.multiple_of((2 * j + c) * PC + i * RT, RT), RT), :] = (
                cen * inv * VEC[0:1, :]
            ).astype(BF)

        loop(PC // RT, body)
        cp_full(AIN, 0, j).start()

    own_x.wait()
    ln1(p, 0)
    ag_ev0[1]()
    ag_ev0[2]()
    for k in range(1, NDP):
        ad_recv(k).wait_recv()
    tot = ADP[0]
    for i in range(1, NDP):
        tot = tot + ADP[i]
    ADS[...] = tot
    for k in range(1, 4):
        adt(k).start()
    ADT[t] = tot
    ag_ev0[3]()
    ag_ev0[4]()
    cp_x_recv().wait_recv()
    ln1(px, 1)
    for e in ag_ev0[5:]:
        e()
    ag_ev1 = ag_events(1)
    ag_ev1[0]()
    for k in range(1, 4):
        adt_recv(k).wait_recv()
    SC = ADT.shape[2] // 2
    for tt in range(4):
        VEC[1:2, SC * tt : SC * (tt + 1)] = 1.0 + ADT[tt, pl.ds(p, 1), 0:SC]
        VEC[2:3, SC * tt : SC * (tt + 1)] = ADT[tt, pl.ds(p, 1), SC : 2 * SC]
    for j in range(2):
        cp_full_recv(AIN, 0, j).wait_recv()
    ag_done(0)

    def wfull(k, j, cols=None):
        v = W[k, j] if cols is None else W[k, j, :, :, cols]
        return v.reshape(D, v.shape[-1])

    HT = T // 2

    def qkv_body(i):
        j, h = lax.div(i, 2), lax.rem(i, 2)
        r = pl.ds(pl.multiple_of(h * HT, HT), HT)
        res = mm(AIN[r, :], wfull(0, j, pl.ds(0, 640)))
        cos, sin = cos_t[r, :], sin_t[r, :]
        rot = []
        for n in range(3):
            x = res[:, 128 * n : 128 * n + 128]
            rot.append(x * cos + swap_halves(x) * sin)
        low = lanes((HT, 128)) < 64
        k1, k2 = pltpu.roll(rot[1], 64, 1), pltpu.roll(rot[2], 64, 1)
        Q[j, r, 0:128] = (rot[0] * 0.125).astype(BF)
        Q[j, r, 128:256] = (rot[1] * 0.125).astype(BF)
        K[j, r, 0:128] = jnp.where(low, k1, k2).astype(BF)
        K[j, r, 128:256] = k2.astype(BF)
        V[j, r, :] = res[:, 384:640].astype(BF)

    loop(4, qkv_body, {2: [ag_ev1[1]], 3: [ag_ev1[2]]})

    pfx = pref[p]
    C0, C1 = 512, 768
    GROUPS = ((0, 512), (512, 256), (768, 256))

    def head_lanes(shape, hh):
        return lax.div(lanes(shape), HD) == hh

    def fwd_body(g):
        j, hh = lax.div(g, 3), lax.rem(g, 3)
        for n, (r0, nr) in enumerate(GROUPS):
            q = jnp.where(head_lanes((nr, 256), hh), Q[j, r0 : r0 + nr, :], jnp.zeros((), BF))
            spans = [(0, C0), (C0, C1), (C1, T)][: n + 1]
            sc = []
            for n2, (k0, k1) in enumerate(spans):
                s = mm_nt(q, K[j, k0:k1, :])
                if n2 == n:
                    row = lax.broadcasted_iota(jnp.int32, s.shape, 0) + r0
                    col = lax.broadcasted_iota(jnp.int32, s.shape, 1) + k0
                    ok = col <= row
                    if n == 0:
                        ok = ok | (col < pfx)
                    s = jnp.where(ok, s, NEG)
                sc.append(s)
            m = jnp.max(sc[0], axis=1, keepdims=True)
            for s in sc[1:]:
                m = jnp.maximum(m, jnp.max(s, axis=1, keepdims=True))
            acc, tot = None, None
            for n2, (k0, k1) in enumerate(spans):
                e = jnp.exp(sc[n2] - m)
                l = jnp.sum(e, axis=1, keepdims=True)
                tot = l if tot is None else tot + l
                eb = e.astype(BF)
                if n2 == 0:
                    EA[g, r0 : r0 + nr, :] = eb
                elif n2 == 1:
                    EB[g, r0 - C0 : r0 - C0 + nr, :] = eb
                else:
                    EC[g] = eb
                o = mm(eb, V[j, k0:k1, :])
                acc = o if acc is None else acc + o
            rinv = 1.0 / tot
            old = RINV[r0 : r0 + nr, :]
            RINV[r0 : r0 + nr, :] = jnp.where(lanes((nr, 128)) == g, rinv, old)
            o = (acc * rinv).astype(BF)
            O[j, r0 : r0 + nr, :] = jnp.where(head_lanes((nr, 256), hh), o, O[j, r0 : r0 + nr, :])

    RINV[...] = jnp.zeros_like(RINV)
    loop(6, fwd_body, {0: [ag_ev1[3]], 1: [ag_ev1[4]], 2: [ag_ev1[5]], 3: [ag_ev1[6]], 5: [ag_ev1[7]]})
    ag_ev2 = ag_events(2)
    ag_ev2[0]()
    cp_dy().start()

    low = lanes((D, 128)) < 64
    for j in range(2):
        w = wfull(0, j, pl.ds(512, 256)).astype(F32)
        t4, t5 = pltpu.roll(w[:, 0:128], 64, 1), pltpu.roll(w[:, 128:256], 64, 1)
        MT[j, :, 0:128] = jnp.where(low, t4, t5).astype(BF)
        MT[j, :, 128:256] = t5.astype(BF)

    def two(ref, j, cc):
        return jnp.concatenate([ref[j, rows_of(0, cc), :], ref[j, rows_of(1, cc), :]], axis=0)

    def split_sum(n, body, nt, send_events=(), own_events=()):
        width = D // nt

        def send(i):
            cols = pl.ds(pl.multiple_of(i * width, width), width)
            v = body(cx, i)
            PS[n % 2, 0, :, cols] = v[0:PC].astype(BF)
            PS[n % 2, 1, :, cols] = v[PC:].astype(BF)

        loop(nt, send, send_events)
        for j in range(2):
            cp_part(n, j).start()

        def own(i):
            cols = pl.ds(pl.multiple_of(i * width, width), width)
            v = body(c, i)
            OWN[0, :, cols] = v[0:PC]
            OWN[1, :, cols] = v[PC:]

        loop(nt, own, own_events)

    def mix_cols(cc, i):
        cols = pl.ds(pl.multiple_of(i * 256, 256), 256)
        return mm_nt(two(O, 0, cc), MT[0, cols, :]) + mm_nt(two(O, 1, cc), MT[1, cols, :])

    split_sum(0, mix_cols, D // 256, {}, {})
    ag_ev2[1]()

    def ln2(j):
        cp_part(0, j).wait_recv()

        def body(i):
            r = pl.ds(pl.multiple_of(i * RT, RT), RT)
            res = X[j, r, :].astype(F32) + OWN[j, r, :] + PR[0, j, r, :].astype(F32)
            RES[j, r, :] = res
            mean, cen, inv = row_stats(res)
            ln = lanes((RT, 128))
            ST[j, r, :] = jnp.where(ln == 0, mean, inv)
            MG[pl.ds(pl.multiple_of((2 * j + c) * PC + i * RT, RT), RT), :] = (
                cen * inv * VEC[1:2, :] + VEC[2:3, :]
            ).astype(BF)

        loop(PC // RT, body)
        cp_full(MG, 1, j).start()

    ln2(0)
    ln2(1)
    ag_ev2[2]()
    ag_done(1)
    for j in range(2):
        cp_full_recv(MG, 1, j).wait_recv()

    CA, CB = 0.7978845608028654, 0.044715

    def tile3(i):
        j, rest = lax.div(i, 6), lax.rem(i, 6)
        h, n = lax.div(rest, 3), lax.rem(rest, 3)
        return j, pl.ds(pl.multiple_of(h * HT, HT), HT), pl.ds(pl.multiple_of(n * 256, 256), 256)

    def up_body(i):
        j, r, cols = tile3(i)
        v = mm(MG[r, :], wfull(1, j, cols))
        v2 = v * v
        th = jnp.tanh(CA * v * (1.0 + CB * v2))
        half = 0.5 + 0.5 * th
        HID[j, r, cols] = (v * half).astype(BF)
        slope = (0.5 * CA) * (1.0 + (3.0 * CB) * v2)
        GP[j, r, cols] = (half + v * (1.0 - th * th) * slope).astype(BF)

    loop(12, up_body, {1: [ag_ev2[3]], 4: [ag_ev2[4]], 7: [ag_ev2[5]]})

    own_dy.wait()
    cp_dy_recv().wait_recv()
    for j in range(2):
        cp_full(DYF, 2, j).start()
    for j in range(2):
        cp_full_recv(DYF, 2, j).wait_recv()

    def wgrad(k, lhs, rhs):
        def body(i):
            j, n = lax.div(i, 3), lax.rem(i, 3)
            cols = pl.ds(pl.multiple_of(n * 256, 256), 256)
            v = mm_tn(lhs[...], rhs[j, :, cols]).astype(BF)
            gr(k)[j, :, :, cols] = v.reshape(NDP, SR, 256)

        return body

    loop(6, wgrad(2, DYF, HID), {1: [ag_ev2[6]], 3: [ag_ev2[7]]})
    rs2, rs1, rs0 = rs_events(2), rs_events(1), rs_events(0)
    rs2[0]()
    ag_done(2)

    def down_cols(cc, i):
        cols = pl.ds(i * (256 // SR) if False else 0, NDP)
        del cols
        return None

    def wrows(k, j, n):
        return W[k, j].reshape(D, W.shape[-1])[n * 256 : n * 256 + 256]

    def ff_split(n, k, src, send_events=(), own_events=()):
        nt = 2
        per = NDP // nt
        width = D // nt

        def body(cc, i):
            w0 = W[k, 0, pl.ds(i * per, per)].reshape(width, W.shape[-1])
            w1 = W[k, 1, pl.ds(i * per, per)].reshape(width, W.shape[-1])
            return mm_nt(two(src, 0, cc), w0) + mm_nt(two(src, 1, cc), w1)

        split_sum(n, body, nt, send_events, own_events)

    ff_split(1, 2, HID)

    def layer_out(jj):
        j = p if jj == 0 else px
        cp_part(1, j).wait_recv()

        def body(i):
            r = pl.ds(pl.multiple_of(i * RT, RT), RT)
            v = (RES[j, r, :] + OWN[j, r, :] + PR[1, j, r, :].astype(F32)).astype(BF)
            if jj == 0:
                lo_out[p, r, :] = v
            else:
                LOS[r, :] = v

        loop(PC // RT, body)
        if jj == 1:
            cp_lo().start()

    def ghid_body(i):
        j, r, cols = tile3(i)
        v = mm(DYF[r, :], wfull(2, j, cols))
        GP[j, r, cols] = (GP[j, r, cols].astype(F32) * v).astype(BF)

    loop(12, ghid_body, {1: [rs2[1], rs2[2]], 6: [rs2[3], rs2[4]]})
    layer_out(1)
    layer_out(0)
    loop(6, wgrad(1, MG, GP), {0: [rs2[5], rs2[6]], 3: [rs2[7], rs2[8]]})
    rs1[0]()
    cp_part(0, 0).wait_send()
    cp_part(0, 1).wait_send()
    ff_split(2, 1, GP)

    def fold(v):
        return jnp.sum(v.reshape(RT // 8, 8, D), axis=0)

    def ln2_back(j):
        cp_part(2, j).wait_recv()

        def body(i):
            r = pl.ds(pl.multiple_of(i * RT, RT), RT)
            rows = pl.ds(pl.multiple_of((2 * j + c) * PC + i * RT, RT), RT)
            gu = OWN[j, r, :] + PR[0, j, r, :].astype(F32)
            st = ST[j, r, :]
            mean, inv = st[:, 0:1], st[:, 1:2]
            nrm = (RES[j, r, :] - mean) * inv
            ACC[0] += fold(gu * nrm)
            ACC[1] += fold(gu)
            g = gu * VEC[1:2, :]
            mg = jnp.mean(g, axis=-1, keepdims=True)
            mc = jnp.mean(g * nrm, axis=-1, keepdims=True)
            out = DYF[rows, :].astype(F32) + inv * (g - mg - nrm * mc)
            RES[j, r, :] = out
            MG[rows, :] = out.astype(BF)

        loop(PC // RT, body)
        cp_full(MG, 3, j).start()

    for j in range(2):
        cp_full(MG, 1, j).wait_send()
    ln2_back(0)
    ln2_back(1)

    def rt(k):
        return rc(SLT.at[tpeer(k)], RTT.at[t], srt.at[0, k], srt.at[1, t], (d, tpeer(k)))

    def rt_recv(k):
        return rc(SLT.at[0], RTT.at[tpeer(k)], srt.at[0, k], srt.at[1, tpeer(k)], DX)

    def gal(k):
        return rc(GA2, GAL.at[d], sgal.at[0, k], sgal.at[1, d], (dpeer(k), t))

    def gal_recv(k):
        return rc(GA2, GAL.at[dpeer(k)], sgal.at[0, k], sgal.at[1, dpeer(k)], DX)

    for n in range(2):
        row = jnp.sum(ACC[n], axis=0, keepdims=True)
        for tt in range(4):
            SLT[tt, n : n + 1, 0:SC] = row[:, SC * tt : SC * (tt + 1)]
    for k in range(1, 4):
        rt(k).start()
    RTT[t] = SLT[t]
    for j in range(2):
        cp_full_recv(MG, 3, j).wait_recv()

    def back_side(jj, ev_fwd, ev_ds):
        j = px if jj == 0 else p

        def gmix(h):
            r = pl.ds(pl.multiple_of(h * HT, HT), HT)
            do = mm(MG[r, :], MT[j]).astype(BF).astype(F32)
            o = O[j, r, :].astype(F32)
            ri = RINV[r, :]
            dl = jnp.zeros((HT, 128), F32)
            for hh in range(3):
                g3 = j * 3 + hh
                rh = jnp.sum(jnp.where(lanes((HT, 128)) == g3, ri, 0.0), axis=1, keepdims=True)
                dm = jnp.where(head_lanes((HT, 256), hh), do * rh, 0.0)
                M3[hh, r, :] = dm.astype(BF)
                dl = jnp.where(lanes((HT, 128)) == hh, jnp.sum(dm * o, axis=1, keepdims=True), dl)
            DEL[r, :] = dl

        loop(2, gmix)

        def e_dot(k0, nk):
            acc = None
            for hh in range(3):
                g = j * 3 + hh
                if k0 < C0:
                    v = mm_tn(EA[g, :, k0 : k0 + nk], M3[hh])
                elif k0 < C1:
                    v = mm_tn(EB[g], M3[hh, C0:T, :])
                else:
                    v = mm_tn(EC[g], M3[hh, C1:T, :])
                acc = v if acc is None else acc + v
            return acc

        KB = ((0, 256), (256, 256), (512, 256), (768, 256))
        for k0, nk in KB:
            GQ[j, k0 : k0 + nk, 384:640] = e_dot(k0, nk).astype(BF)

        def ds_body(hh):
            g = j * 3 + hh
            for n, (r0, nr) in enumerate(GROUPS):
                dm = M3[hh, r0 : r0 + nr, :]
                dl = jnp.sum(
                    jnp.where(lanes((nr, 128)) == hh, DEL[r0 : r0 + nr, :], 0.0), axis=1, keepdims=True
                )
                spans = [(0, C0), (C0, C1), (C1, T)][: n + 1]
                for n2, (k0, k1) in enumerate(spans):
                    dp = mm_nt(dm, V[j, k0:k1, :]) - dl
                    if n2 == 0:
                        EA[g, r0 : r0 + nr, :] = (EA[g, r0 : r0 + nr, :].astype(F32) * dp).astype(BF)
                    elif n2 == 1:
                        e0 = r0 - C0
                        EB[g, e0 : e0 + nr, :] = (EB[g, e0 : e0 + nr, :].astype(F32) * dp).astype(BF)
                    else:
                        EC[g] = (EC[g].astype(F32) * dp).astype(BF)

        loop(3, ds_body, ev_ds)

        for n, (r0, nr) in enumerate(GROUPS):
            acc = None
            for hh in range(3):
                g = j * 3 + hh
                for n2, (k0, k1) in enumerate([(0, C0), (C0, C1), (C1, T)][: n + 1]):
                    kk = K[j, k0:k1, :]
                    km = jnp.where(head_lanes(kk.shape, hh), kk, jnp.zeros((), BF))
                    if n2 == 0:
                        s = EA[g, r0 : r0 + nr, :]
                    elif n2 == 1:
                        s = EB[g, r0 - C0 : r0 - C0 + nr, :]
                    else:
                        s = EC[g]
                    v = mm(s, km)
                    acc = v if acc is None else acc + v
            acc = acc * 0.125
            cos, sin = cos_t[r0 : r0 + nr, :], sin_t[r0 : r0 + nr, :]
            for n2 in range(2):
                x = acc[:, 128 * n2 : 128 * n2 + 128]
                GQ[j, r0 : r0 + nr, 128 * n2 : 128 * n2 + 128] = (x * cos - swap_halves(x) * sin).astype(BF)
        for hh in range(3):
            qq = Q[j]
            M3[hh] = jnp.where(head_lanes(qq.shape, hh), qq, jnp.zeros((), BF))
        for k0, nk in KB:
            v = e_dot(k0, nk)
            cos, sin = cos_t[k0 : k0 + nk, :], sin_t[k0 : k0 + nk, :]
            un = []
            for n2 in range(2):
                x = v[:, 128 * n2 : 128 * n2 + 128]
                un.append(pltpu.roll(x * cos - swap_halves(x) * sin, 64, 1))
            lowk = lanes((nk, 128)) < 64
            old = GQ[j, k0 : k0 + nk, 128:256].astype(F32)
            GQ[j, k0 : k0 + nk, 128:256] = jnp.where(lowk, old, un[0]).astype(BF)
            GQ[j, k0 : k0 + nk, 256:384] = jnp.where(lowk, un[0], un[1]).astype(BF)

        g0 = gr(0)
        for n in range(2):
            v = mm_tn(AIN[...], GQ[j, :, 256 * n : 256 * n + 256]).astype(BF)
            g0[j, :, :, 256 * n : 256 * n + 256] = v.reshape(NDP, SR, 256)
        gv = mm_tn(AIN[...], GQ[j, :, 512:640])
        gm = mm_tn(MG[...], O[j])
        m0, m1 = pltpu.roll(gm[:, 0:128], 64, 1), pltpu.roll(gm[:, 128:256], 64, 1)
        lowd = lanes((D, 128)) < 64
        g0[j, :, :, 512:640] = jnp.where(lowd, gv, m0).astype(BF).reshape(NDP, SR, 128)
        g0[j, :, :, 640:768] = jnp.where(lowd, m0, m1).astype(BF).reshape(NDP, SR, 128)

    ag_sent(2)
    back_side(0, {}, {0: [rs2[9], rs1[1], rs1[2]], 1: [rs1[3], rs1[4]]})
    rs1[5]()
    rs1[6]()

    for k in range(1, 4):
        rt_recv(k).wait_recv()
    for s in range(2):
        v = RTT[2 * s] + RTT[2 * s + 1]
        for n in range(2):
            GA2[n, s : s + 1, :] = v[n : n + 1, :]
    for k in range(1, NDP):
        gal(k).start()
    GAL[d] = GA2[...]

    back_side(1, {}, {0: [rs1[7], rs1[8]], 2: [rs1[9]]})
    rs0[0]()

    for k in range(1, NDP):
        gal_recv(k).wait_recv()
    feat = SMR[...].reshape(NDP * 8, 128)
    for n in range(2):
        v = lax.dot_general(
            feat,
            GAL[:, n].reshape(NDP * 8, 256),
            (((0,), (0,)), ((), ())),
            preferred_element_type=F32,
            precision=lax.Precision.HIGHEST,
        )
        ga_out[n] = v[0:SR, 0:SC]

    cp_part(1, 0).wait_send()
    cp_part(1, 1).wait_send()

    def in_cols(cc, i):
        per = NDP // 2
        acc = None
        for j in range(2):
            w = W[0, j, pl.ds(i * per, per), :, pl.ds(0, 640)].reshape(D // 2, 640)
            v = mm_nt(two(GQ, j, cc), w)
            acc = v if acc is None else acc + v
        return acc

    split_sum(3, in_cols, 2, {}, {})
    for e in rs0[1:5]:
        e()

    def ln1_back(jj):
        j = px if jj == 0 else p
        cp_part(3, j).wait_recv()

        def body(i):
            r = pl.ds(pl.multiple_of(i * RT, RT), RT)
            gi = OWN[j, r, :] + PR[1, j, r, :].astype(F32)
            mean, cen, inv = row_stats(X[j, r, :].astype(F32))
            nrm = cen * inv
            ACC[2] += fold(gi * nrm)
            g = gi * VEC[0:1, :]
            mg = jnp.mean(g, axis=-1, keepdims=True)
            mc = jnp.mean(g * nrm, axis=-1, keepdims=True)
            out = (RES[j, r, :] + inv * (g - mg - nrm * mc)).astype(BF)
            if jj == 0:
                IGS[r, :] = out
            else:
                ig_out[p, r, :] = out

        loop(PC // RT, body)
        if jj == 0:
            cp_ig().start()

    ln1_back(0)
    ln1_back(1)

    def gt(k):
        return rc(GGT.at[t], GGT.at[t], sgt.at[0, k], sgt.at[1, t], (d, tpeer(k)))

    def gt_recv(k):
        return rc(GGT.at[t], GGT.at[tpeer(k)], sgt.at[0, k], sgt.at[1, tpeer(k)], DX)

    def grd(k):
        return rc(GGS.at[dpeer(k)], GGR.at[d], sgr.at[0, k], sgr.at[1, d], (dpeer(k), t))

    def grd_recv(k):
        return rc(GGS.at[0], GGR.at[dpeer(k)], sgr.at[0, k], sgr.at[1, dpeer(k)], DX)

    GGT[t] = ACC[2]
    for k in range(1, 4):
        gt(k).start()
    for e in rs0[5:9]:
        e()
    for k in range(1, 4):
        gt_recv(k).wait_recv()
    row = jnp.sum(GGT[0] + GGT[1] + GGT[2] + GGT[3], axis=0, keepdims=True)
    for i in range(NDP):
        GGS[i, 0:1, 0:SR] = row[:, SR * i : SR * (i + 1)]
    for k in range(1, NDP):
        grd(k).start()
    GGR[d] = GGS[d]
    for k in range(1, NDP):
        grd_recv(k).wait_recv()
    tot = GGR[0]
    for i in range(1, NDP):
        tot = tot + GGR[i]
    gg_out[...] = tot
    rs0[9]()

    cp_x().wait_send()
    cp_dy().wait_send()
    cp_lo().wait_send()
    cp_lo_recv().wait_recv()
    cp_ig().wait_send()
    cp_ig_recv().wait_recv()
    for j in range(2):
        cp_full(AIN, 0, j).wait_send()
        cp_full(DYF, 2, j).wait_send()
        cp_full(MG, 3, j).wait_send()
        cp_part(2, j).wait_send()
        cp_part(3, j).wait_send()
    ag_sent(0)
    ag_sent(1)
    for k in range(3):
        rs_sent(k)
    for k in range(1, NDP):
        sm(k).wait_send()
        ad(k).wait_send()
        gal(k).wait_send()
        grd(k).wait_send()
    for k in range(1, 4):
        adt(k).wait_send()
        rt(k).wait_send()
        gt(k).wait_send()


def fused_local(layer_in, prefix_len, time_step, norm_gain, qkv_weight, mix_weight, ada_weight, up_weight, down_weight, out_grad):
    ndp = lax.axis_size("dp")
    _, pc, width = layer_in.shape
    length = pc * 4
    sr = width // ndp
    nz = ndp // 2
    ha = (2 * sr) // 3
    temb = time_features(time_step, width).astype(jnp.bfloat16).astype(jnp.float32)
    feat = jnp.moveaxis(temb.reshape(2, ndp, sr), 0, 1)
    gain = jnp.broadcast_to(norm_gain.astype(jnp.float32)[None, None], (ndp, 1, sr))
    small = jnp.concatenate([feat, gain], axis=1)
    small = jnp.pad(small, ((0, 0), (0, 5), (0, 128 - sr)))
    wsl = jnp.stack(
        [
            jnp.concatenate([qkv_weight.reshape(sr, -1), mix_weight.T], axis=1),
            up_weight,
            down_weight.T,
        ]
    )
    sc = ada_weight.shape[2]
    adaw = jnp.pad(ada_weight.reshape(sr, 2 * sc), ((0, 128 - sr), (0, 0)))
    cosn, sinn = rope_tables(length)
    dims = (ndp, nz, sr, width, length, pc)
    bf, f32 = jnp.bfloat16, jnp.float32
    vm = pltpu.VMEM
    dma = pltpu.SemaphoreType.DMA
    scratch = [
        vm((3, 2, ndp, sr, width), bf),
        vm((2, pc, width), bf),
        vm((length, width), bf),
        vm((length, width), bf),
        vm((length, width), bf),
        vm((2, length, 256), bf),
        vm((2, length, 256), bf),
        vm((2, length, 256), bf),
        vm((6, length, 512), bf),
        vm((6, 512, 256), bf),
        vm((6, 256, 256), bf),
        vm((2, length, 256), bf),
        vm((length, 128), f32),
        vm((2, width, 256), bf),
        vm((2, pc, width), f32),
        vm((2, pc, 128), f32),
        vm((2, pc, width), f32),
        vm((2, 2, pc, width), bf),
        vm((2, 2, pc, width), bf),
        vm((2, length, width), bf),
        vm((2, length, width), bf),
        vm((3, length, 256), bf),
        vm((length, 128), f32),
        vm((2, length, 640), bf),
        vm((2, 2, ndp, sr, width), bf),
        vm((nz, ha, width), bf),
        vm((nz, sr - ha, width), bf),
        vm((nz, sr, width), bf),
        vm((nz, sr, width), bf),
        vm((3, nz, sr, width), bf),
        vm((pc, width), bf),
        vm((pc, width), bf),
        vm((ndp, 8, 128), f32),
        vm((ndp, 8, 2 * sc), f32),
        vm((ndp, 8, 2 * sc), f32),
        vm((8, 2 * sc), f32),
        vm((4, 8, 2 * sc), f32),
        vm((8, width), f32),
        vm((3, 8, width), f32),
        vm((4, 8, 256), f32),
        vm((4, 8, 256), f32),
        vm((2, 8, 256), f32),
        vm((ndp, 2, 8, 256), f32),
        vm((4, 8, width), f32),
        vm((ndp, 8, 128), f32),
        vm((ndp, 8, 128), f32),
        dma((4, 2)),
        dma((2, 3, nz)),
        dma((2, 3, nz)),
        dma((2, 3, nz)),
        dma((2, 3, nz)),
        dma((2, 3, nz)),
        dma((2, 3, nz)),
        dma((2, 3, nz)),
        dma((2, 3, nz)),
        dma((2, 3, nz)),
        dma((2, 3, nz)),
        dma((2, 8, 2)),
        dma((2, ndp)),
        dma((2, ndp)),
        dma((2, 4)),
        dma((2, 4)),
        dma((2, ndp)),
        dma((2, 4)),
        dma((2, ndp)),
        dma((2,)),
    ]
    vspec = pl.BlockSpec(memory_space=pltpu.VMEM)
    lo, ig, gw, ga, gg = pl.pallas_call(
        functools.partial(layer_kernel, dims),
        out_shape=(
            jax.ShapeDtypeStruct((2, pc, width), bf),
            jax.ShapeDtypeStruct((2, pc, width), bf),
            jax.ShapeDtypeStruct((3, sr, width), f32),
            jax.ShapeDtypeStruct((2, sr, sc), f32),
            jax.ShapeDtypeStruct((8, 128), f32),
        ),
        in_specs=[pl.BlockSpec(memory_space=pltpu.SMEM), vspec] + [pl.BlockSpec(memory_space=pl.ANY)] * 2 + [vspec] * 4,
        out_specs=(vspec,) * 5,
        scratch_shapes=scratch,
        compiler_params=pltpu.CompilerParams(
            collective_id=0, has_side_effects=True, vmem_limit_bytes=67043328
        ),
        name="layer_step",
    )(prefix_len, small, layer_in, out_grad, wsl, adaw, cosn, sinn)
    qm = 3 * sc
    return (
        lo,
        ig,
        gg[0, :sr],
        gw[0, :, :qm].reshape(sr, 3, sc),
        gw[0, :, qm:].T,
        jnp.moveaxis(ga, 0, 1),
        gw[1],
        gw[2].T,
    )


def rope_tables(length):
    half = HD // 2
    freq = np.exp(np.arange(half, dtype=np.float32) * np.float32(-math.log(10000.0) / half)).astype(np.float32)
    ang = np.arange(length, dtype=np.float32)[:, None] * freq[None, :]
    cos, sin = np.cos(ang).astype(np.float32), np.sin(ang).astype(np.float32)
    return np.concatenate([cos] * 4, axis=1), np.concatenate([-sin, sin] * 2, axis=1)


def one_kernel(mesh, shapes=None):
    return mesh.shape["tensor"] == 4 and mesh.shape["dp"] == 8


def solution(mesh):
    return jax.shard_map(
        fused_local if one_kernel(mesh) else local,
        mesh=mesh,
        in_specs=(
            P("dp", "tensor", None),
            P("dp"),
            P("dp"),
            P("dp"),
            P("dp", None, "tensor"),
            P("tensor", "dp"),
            P("dp", None, "tensor"),
            P("dp", "tensor"),
            P("tensor", "dp"),
            P("dp", "tensor", None),
        ),
        out_specs=(
            P("dp", "tensor", None),
            P("dp", "tensor", None),
            P("dp"),
            P("dp", None, "tensor"),
            P("tensor", "dp"),
            P("dp", None, "tensor"),
            P("dp", "tensor"),
            P("tensor", "dp"),
        ),
        check_vma=False,
    )
```

```python
import functools
import math

import jax
import jax.numpy as jnp
import numpy as np
from jax import lax
from jax.experimental import pallas as pl
from jax.experimental.pallas import tpu as pltpu
from jax.sharding import PartitionSpec as P

HD = 64


EPS = 1e-05


def cut_along(shard, dim, size):
    dims = shard.shape
    parts = shard.reshape(*dims[:dim], size, dims[dim] // size, *dims[dim + 1 :])
    return jnp.moveaxis(parts, dim, 0)


def sum_at_owner(shard, axis, dim):
    size = lax.axis_size(axis)
    parts = lax.all_to_all(cut_along(shard, dim, size), axis, 0, 0, tiled=True)
    return jnp.sum(parts.astype(jnp.float32), axis=0)


def side_by_side(arrays, axis, dim, along):
    widths = [math.prod(a.shape[along:]) for a in arrays]
    both = jnp.concatenate(
        [a.reshape(*a.shape[:along], w) for a, w in zip(arrays, widths)], axis=along
    )
    filled = sum_at_owner(both, axis, dim)
    parts = jnp.split(filled, [sum(widths[:k]) for k in range(1, len(widths))], axis=along)
    return tuple(
        (b.reshape(*filled.shape[:along], *a.shape[along:]) for a, b in zip(arrays, parts))
    )


def sent_together(arrays, axis, dim, along):
    widths = [a.shape[along] for a in arrays]
    both = jnp.concatenate(arrays, axis=along)
    filled = sum_at_owner(both, axis, dim)
    return tuple(jnp.split(filled, [sum(widths[:k]) for k in range(1, len(widths))], axis=along))


def normalize(values):
    mean_val = jnp.mean(values, axis=-1, keepdims=True)
    centred = values - mean_val
    inv_std = lax.rsqrt(jnp.mean(centred * centred, axis=-1, keepdims=True) + EPS)
    return (centred * inv_std, inv_std)


def norm_back(grad_norm, normed, inv_std):
    mean_grad = jnp.mean(grad_norm, axis=-1, keepdims=True)
    mean_cross = jnp.mean(grad_norm * normed, axis=-1, keepdims=True)
    return inv_std * (grad_norm - mean_grad - normed * mean_cross)


def gelu_tanh(values):
    return (
        0.5
        * values
        * (1.0 + jnp.tanh(0.7978845608028654 * (values + 0.044715 * values * values * values)))
    )


def time_features(time_step, feat_width):
    half_width = feat_width // 2
    inv_freq = jnp.exp(
        jnp.arange(half_width, dtype=jnp.float32) * (-math.log(10000.0) / half_width)
    )
    angles = time_step.astype(jnp.float32)[:, None] * inv_freq[None, :]
    return jnp.concatenate([jnp.sin(angles), jnp.cos(angles)], axis=1)


def rotary_tables(length, head_size):
    half_size = head_size // 2
    inv_freq = jnp.exp(jnp.arange(half_size, dtype=jnp.float32) * (-math.log(10000.0) / half_size))
    angles = jnp.arange(length, dtype=jnp.float32)[:, None] * inv_freq[None, :]
    return (jnp.cos(angles)[:, None, :], jnp.sin(angles)[:, None, :])


def rotate(values, cosine, sine_tab):
    half_size = values.shape[-1] // 2
    first_half = values[..., :half_size]
    second = values[..., half_size:]
    return jnp.concatenate(
        [first_half * cosine - second * sine_tab, second * cosine + first_half * sine_tab], axis=-1
    )


def unrotate(grad_rot, cosine, sine_tab):
    half_size = grad_rot.shape[-1] // 2
    first_half = grad_rot[..., :half_size]
    second = grad_rot[..., half_size:]
    return jnp.concatenate(
        [first_half * cosine + second * sine_tab, second * cosine - first_half * sine_tab], axis=-1
    )


def allowed_mask(row_start, block_rows, length, prefix_one):
    row_pos = row_start + jnp.arange(block_rows, dtype=jnp.int32)
    key_pos = jnp.arange(length, dtype=jnp.int32)
    return (key_pos[None, :] <= row_pos[:, None]) | (key_pos[None, :] < prefix_one)


def block_scores(q_blk, k_rot, row_start, prefix_one):
    block_rows = q_blk.shape[0]
    score_scale = 1.0 / math.sqrt(q_blk.shape[2])
    scores = (
        jnp.einsum("qhd,khd->hqk", q_blk, k_rot, preferred_element_type=jnp.float32) * score_scale
    )
    mask_blk = allowed_mask(row_start, block_rows, k_rot.shape[0], prefix_one)
    return jnp.where(mask_blk[None], scores, -1e30)


def attend_forward(q_rot, k_rot, v_heads, prefix_one, block_rows):
    length, num_heads, head_size = q_rot.shape
    block_count = length // block_rows
    q_blocks = q_rot.reshape(block_count, block_rows, num_heads, head_size)
    starts = jnp.arange(block_count, dtype=jnp.int32) * block_rows

    def one_block(block_in):
        q_blk, row_start = block_in
        scores = block_scores(q_blk, k_rot, row_start, prefix_one)
        row_max = jnp.max(scores, axis=-1, keepdims=True)
        exp_scores = jnp.exp(scores - row_max)
        exp_total = jnp.sum(exp_scores, axis=-1, keepdims=True)
        attn_prob = (exp_scores / exp_total).astype(jnp.bfloat16)
        attn_mix = jnp.einsum(
            "hqk,khd->qhd", attn_prob, v_heads, preferred_element_type=jnp.float32
        )
        return (attn_mix, (row_max + jnp.log(exp_total))[..., 0])

    attn_mix, log_sum = lax.map(one_block, (q_blocks, starts))
    return (attn_mix.reshape(length, num_heads, head_size), log_sum)


def attend_backward(q_rot, k_rot, v_heads, grad_mix, log_sum, prefix_one, block_rows):
    length, num_heads, head_size = q_rot.shape
    block_count = length // block_rows
    score_scale = 1.0 / math.sqrt(head_size)
    q_blocks = q_rot.reshape(block_count, block_rows, num_heads, head_size)
    g_blocks = grad_mix.reshape(block_count, block_rows, num_heads, head_size)
    starts = jnp.arange(block_count, dtype=jnp.int32) * block_rows

    def one_block(grad_carry, block_in):
        grad_k, grad_v = grad_carry
        q_blk, g_blk, lse_blk, row_start = block_in
        scores = block_scores(q_blk, k_rot, row_start, prefix_one)
        attn_soft = jnp.exp(scores - lse_blk[..., None])
        attn_prob = attn_soft.astype(jnp.bfloat16)
        grad_p = jnp.einsum("qhd,khd->hqk", g_blk, v_heads, preferred_element_type=jnp.float32)
        row_delta = jnp.sum(grad_p * attn_soft, axis=-1, keepdims=True)
        grad_s = (attn_soft * (grad_p - row_delta)).astype(jnp.bfloat16)
        grad_q = (
            jnp.einsum("hqk,khd->qhd", grad_s, k_rot, preferred_element_type=jnp.float32)
            * score_scale
        )
        grad_k = (
            grad_k
            + jnp.einsum("hqk,qhd->khd", grad_s, q_blk, preferred_element_type=jnp.float32)
            * score_scale
        )
        grad_v = grad_v + jnp.einsum(
            "hqk,qhd->khd", attn_prob, g_blk, preferred_element_type=jnp.float32
        )
        return ((grad_k, grad_v), grad_q)

    zero_kv = jnp.zeros((length, num_heads, head_size), jnp.float32)
    carried, grad_q = lax.scan(one_block, (zero_kv, zero_kv), (q_blocks, g_blocks, log_sum, starts))
    return (grad_q.reshape(length, num_heads, head_size), carried[0], carried[1])


def seq_gather(piece):
    return lax.all_gather(piece, "tensor", axis=0, tiled=True)


def seq_sum(partial_rows):
    return lax.psum_scatter(
        partial_rows.astype(jnp.bfloat16), "tensor", scatter_dimension=0, tiled=True
    ).astype(jnp.float32)


def fetch_weights(norm_gain, qkv_weight, ada_weight, up_weight, mix_weight, down_weight):
    row_parts = (
        lax.all_gather(norm_gain, "dp", axis=0, tiled=True),
        lax.all_gather(qkv_weight, "dp", axis=0, tiled=True),
        lax.all_gather(ada_weight, "dp", axis=0, tiled=True),
        lax.all_gather(up_weight, "dp", axis=0, tiled=True),
    )
    col_parts = (
        lax.all_gather(mix_weight, "dp", axis=1, tiled=True),
        lax.all_gather(down_weight, "dp", axis=1, tiled=True),
    )
    return tuple(row_parts) + tuple(col_parts)


def reduce_owned(row_terms, col_terms):
    row_owned = side_by_side(
        (
            row_terms[0].astype(jnp.bfloat16),
            row_terms[1].astype(jnp.bfloat16),
            row_terms[2].astype(jnp.bfloat16),
            row_terms[3].astype(jnp.bfloat16),
        ),
        "dp",
        0,
        1,
    )
    col_owned = sent_together(
        (col_terms[0].astype(jnp.bfloat16), col_terms[1].astype(jnp.bfloat16)), "dp", 1, 0
    )
    return (tuple(row_owned), tuple(col_owned))


def add_tree(first_sum, second_sum):
    if first_sum is None:
        return second_sum
    return jax.tree.map(jnp.add, first_sum, second_sum)


def local(
    layer_in,
    prefix_len,
    time_step,
    norm_gain,
    qkv_weight,
    mix_weight,
    ada_weight,
    up_weight,
    down_weight,
    out_grad,
):
    micro_count, piece_len, model_width = layer_in.shape
    length = piece_len * lax.axis_size("tensor")
    block_rows = min(512, length)
    tensor_idx = lax.axis_index("tensor")
    col_width = ada_weight.shape[2]
    time_emb = time_features(time_step, model_width).astype(jnp.bfloat16)
    cosine, sine_tab = rotary_tables(length, HD)
    owned = None
    outputs = []
    in_grads = []
    for micro_idx in range(micro_count):
        current = fetch_weights(
            norm_gain, qkv_weight, ada_weight, up_weight, mix_weight, down_weight
        )
        gain_full, wq_full, wada_full, wup_full, wmix_full, wdown_full = current
        gain_f = gain_full.astype(jnp.float32)
        x_piece = layer_in[micro_idx].astype(jnp.float32)
        prefix_one = prefix_len[micro_idx]
        normed1, inv1 = normalize(x_piece)
        attn_in = seq_gather((normed1 * gain_f).astype(jnp.bfloat16))
        qkv_all = jnp.einsum("ld,dch->lch", attn_in, wq_full, preferred_element_type=jnp.float32)
        num_heads = qkv_all.shape[2] // HD
        q_rot = rotate(qkv_all[:, 0].reshape(length, num_heads, HD), cosine, sine_tab).astype(
            jnp.bfloat16
        )
        k_rot = rotate(qkv_all[:, 1].reshape(length, num_heads, HD), cosine, sine_tab).astype(
            jnp.bfloat16
        )
        v_heads = qkv_all[:, 2].reshape(length, num_heads, HD).astype(jnp.bfloat16)
        attn_mix, log_sum = attend_forward(q_rot, k_rot, v_heads, prefix_one, block_rows)
        mix_low = attn_mix.reshape(length, num_heads * HD).astype(jnp.bfloat16)
        resid = x_piece + seq_sum(jnp.dot(mix_low, wmix_full, preferred_element_type=jnp.float32))
        normed2, inv2 = normalize(resid)
        ada_cols = jnp.einsum(
            "d,dch->ch", time_emb[micro_idx], wada_full, preferred_element_type=jnp.float32
        )
        ada_all = lax.all_gather(ada_cols, "tensor", axis=1, tiled=True)
        mlp_rows = (normed2 * (1.0 + ada_all[0]) + ada_all[1]).astype(jnp.bfloat16)
        mlp_in = seq_gather(mlp_rows)
        gate_pre = jnp.dot(mlp_in, wup_full, preferred_element_type=jnp.float32)
        hidden_low = gelu_tanh(gate_pre).astype(jnp.bfloat16)
        mlp_piece = seq_sum(jnp.dot(hidden_low, wdown_full, preferred_element_type=jnp.float32))
        outputs.append((resid + mlp_piece).astype(jnp.bfloat16))
        current = fetch_weights(
            norm_gain, qkv_weight, ada_weight, up_weight, mix_weight, down_weight
        )
        gain_full, wq_full, wada_full, wup_full, wmix_full, wdown_full = current
        grad_top = out_grad[micro_idx].astype(jnp.float32)
        gelu_out, gelu_back = jax.vjp(gelu_tanh, gate_pre)
        grad_mlp = seq_gather(out_grad[micro_idx])
        grad_hidden = jnp.einsum(
            "ld,fd->lf", grad_mlp, wdown_full, preferred_element_type=jnp.float32
        )
        down_term = jnp.einsum(
            "lf,ld->fd", hidden_low, grad_mlp, preferred_element_type=jnp.float32
        )
        grad_gate = gelu_back(grad_hidden)[0].astype(jnp.bfloat16)
        up_term = jnp.einsum("ld,lf->df", mlp_in, grad_gate, preferred_element_type=jnp.float32)
        grad_u = seq_sum(
            jnp.einsum("lf,df->ld", grad_gate, wup_full, preferred_element_type=jnp.float32)
        )
        ada_term = jnp.stack([jnp.sum(grad_u * normed2, axis=0), jnp.sum(grad_u, axis=0)])
        grad_res = grad_top + norm_back(grad_u * (1.0 + ada_all[0]), normed2, inv2)
        grad_attn = seq_gather(grad_res.astype(jnp.bfloat16))
        grad_mix = jnp.einsum(
            "ld,hd->lh", grad_attn, wmix_full, preferred_element_type=jnp.float32
        ).astype(jnp.bfloat16)
        mix_term = jnp.einsum("lh,ld->hd", mix_low, grad_attn, preferred_element_type=jnp.float32)
        grad_q, grad_k, grad_v = attend_backward(
            q_rot,
            k_rot,
            v_heads,
            grad_mix.reshape(length, num_heads, HD),
            log_sum,
            prefix_one,
            block_rows,
        )
        grad_qkv = jnp.stack(
            [
                unrotate(grad_q, cosine, sine_tab).reshape(length, num_heads * HD),
                unrotate(grad_k, cosine, sine_tab).reshape(length, num_heads * HD),
                grad_v.reshape(length, num_heads * HD),
            ],
            axis=1,
        ).astype(jnp.bfloat16)
        qkv_term = jnp.einsum("ld,lch->dch", attn_in, grad_qkv, preferred_element_type=jnp.float32)
        grad_a = seq_sum(
            jnp.einsum("lch,dch->ld", grad_qkv, wq_full, preferred_element_type=jnp.float32)
        )
        gain_part = jnp.sum(grad_a * normed1, axis=0)
        ada_sum, gain_sum = lax.psum((ada_term, gain_part), "tensor")
        ada_slice = lax.dynamic_slice_in_dim(ada_sum, tensor_idx * col_width, col_width, 1)
        ada_w_term = time_emb[micro_idx].astype(jnp.float32)[:, None, None] * ada_slice[None]
        in_grads.append((grad_res + norm_back(grad_a * gain_f, normed1, inv1)).astype(jnp.bfloat16))
        row_terms = (gain_sum, qkv_term, ada_w_term, up_term)
        col_terms = (mix_term, down_term)
        owned = add_tree(owned, reduce_owned(row_terms, col_terms))
    row_owned, col_owned = owned
    return (
        jnp.stack(outputs),
        jnp.stack(in_grads),
        row_owned[0],
        row_owned[1],
        col_owned[0],
        row_owned[2],
        row_owned[3],
        col_owned[1],
    )


MESH_ID = pl.DeviceIdType.MESH
BF = jnp.bfloat16
F32 = jnp.float32
NEG = -1e30


def mm(a, b):
    return lax.dot_general(a, b, (((1,), (0,)), ((), ())), preferred_element_type=F32)


def mm_nt(a, b):
    return lax.dot_general(a, b, (((1,), (1,)), ((), ())), preferred_element_type=F32)


def mm_tn(a, b):
    return lax.dot_general(a, b, (((0,), (0,)), ((), ())), preferred_element_type=F32)


def lanes(shape):
    return lax.broadcasted_iota(jnp.int32, shape, len(shape) - 1)


def row_stats(x):
    mean = jnp.mean(x, axis=-1, keepdims=True)
    cen = x - mean
    inv = lax.rsqrt(jnp.mean(cen * cen, axis=-1, keepdims=True) + EPS)
    return mean, cen, inv


def swap_halves(x):
    low = lax.rem(lanes(x.shape), HD) < HD // 2
    return jnp.where(low, pltpu.roll(x, 128 - HD // 2, 1), pltpu.roll(x, HD // 2, 1))


def layer_kernel(
    dims,
    pref,
    small,
    xin,
    dyin,
    wsl,
    adaw,
    cos_t,
    sin_t,
    lo_out,
    ig_out,
    gw_out,
    ga_out,
    gg_out,
    W,
    X,
    DYF,
    AIN,
    MG,
    Q,
    K,
    V,
    EA,
    EB,
    EC,
    O,
    RINV,
    MT,
    RES,
    ST,
    OWN,
    PS,
    PR,
    HID,
    GP,
    M3,
    DEL,
    GQ,
    G,
    LAND2A,
    LAND2,
    LAND1,
    LOS,
    IGS,
    SMR,
    ADP,
    ADL,
    ADS,
    ADT,
    VEC,
    ACC,
    SLT,
    RTT,
    GA2,
    GAL,
    GGT,
    GGS,
    GGR,
    sx,
    sag,
    srs,
    cred,
    score,
    ssm,
    sad,
    sadt,
    srt,
    sgal,
    sgt,
    sgr,
    sloc,
):
    NDP, NZ, SR, D, T, PC = dims
    d = lax.axis_index("dp")
    t = lax.axis_index("tensor")
    z, y = lax.div(d, 2), lax.rem(d, 2)
    p, c = lax.div(t, 2), lax.rem(t, 2)
    px, yx, cx = 1 - p, 1 - y, 1 - c
    DX, DY_, DC = (d, px * 2 + c), (z * 2 + yx, t), (d, p * 2 + cx)

    def zi(dz):
        return lax.rem(z + dz, NZ)

    def dpeer(k):
        return lax.rem(d + k, NDP)

    def tpeer(k):
        return lax.rem(t + k, 4)

    def rc(src, dst, s, r, dev):
        return pltpu.make_async_remote_copy(
            src_ref=src, dst_ref=dst, send_sem=s, recv_sem=r, device_id=dev, device_id_type=MESH_ID
        )

    bar = pltpu.get_barrier_semaphore()
    for k in range(1, NDP):
        pl.semaphore_signal(bar, 1, device_id=(dpeer(k), t), device_id_type=MESH_ID)
    for k in range(1, 4):
        pl.semaphore_signal(bar, 1, device_id=(d, tpeer(k)), device_id_type=MESH_ID)
    pl.semaphore_wait(bar, NDP - 1 + 3)

    def cp_x():
        return rc(xin.at[px], X.at[p], sx.at[0, 0], sx.at[0, 1], DX)

    def cp_x_recv():
        return rc(xin.at[px], X.at[px], sx.at[0, 0], sx.at[0, 1], DX)

    def rows_of(j, cc):
        return pl.ds(pl.multiple_of((2 * j + cc) * PC, PC), PC)

    def cp_dy():
        return rc(dyin.at[px], DYF.at[rows_of(p, c)], sx.at[1, 0], sx.at[1, 1], DX)

    def cp_dy_recv():
        return rc(dyin.at[px], DYF.at[rows_of(px, c)], sx.at[1, 0], sx.at[1, 1], DX)

    def cp_lo():
        return rc(LOS, lo_out.at[p], sx.at[2, 0], sx.at[2, 1], DX)

    def cp_lo_recv():
        return rc(LOS, lo_out.at[px], sx.at[2, 0], sx.at[2, 1], DX)

    def cp_ig():
        return rc(IGS, ig_out.at[p], sx.at[3, 0], sx.at[3, 1], DX)

    def cp_ig_recv():
        return rc(IGS, ig_out.at[px], sx.at[3, 0], sx.at[3, 1], DX)

    def cp_full(buf, n, j):
        return rc(buf.at[rows_of(j, c)], buf.at[rows_of(j, c)], score.at[0, n, j], score.at[1, n, j], DC)

    def cp_full_recv(buf, n, j):
        return rc(buf.at[rows_of(j, cx)], buf.at[rows_of(j, cx)], score.at[0, n, j], score.at[1, n, j], DC)

    PSET = (0, 1, 1, 0)

    def cp_part(n, j):
        s = PSET[n]
        return rc(PS.at[s, j], PR.at[s, j], score.at[0, 4 + n, j], score.at[1, 4 + n, j], DC)

    RX, R1 = SR // 6, 3 * (SR // 4)
    NQ = SR - R1
    P1, PX, PY, P2 = pl.ds(0, R1), pl.ds(0, RX), pl.ds(RX, R1 - RX), pl.ds(R1, NQ)
    zhalf = lax.div(z, 2)
    zs = (z + 1 - 2 * lax.rem(z, 2), 2 - zhalf, 3 * (1 - zhalf), z)
    mid = (z == 1) | (z == 2)
    end = jnp.logical_not(mid)

    def zdev(zq):
        return (zq * 2 + y, t)

    def when(cond, fn):
        pl.when(cond)(fn)

    def ag_z(k, o):
        r = W.at[k, p, z, y, P1]
        return rc(wsl.at[k, P1], r, sag.at[0, 0, k, o], sag.at[1, 0, k, z], zdev(zs[o]))

    def ag_far(k):
        r = W.at[k, p, zs[2], y, P1]
        return rc(r, r, sag.at[0, 0, k, 3], sag.at[1, 0, k, zs[2]], zdev(zs[0]))

    def ag_z_recv(k, zq):
        r = W.at[k, p, zq, y, P1]
        return rc(r, r, sag.at[0, 0, k, 0], sag.at[1, 0, k, zq], DX)

    def ag_x(k, zq, own=False):
        r = W.at[k, p, zq, y, P1]
        return rc(wsl.at[k, P1] if own else r, r, sag.at[0, 1, k, zq], sag.at[1, 1, k, zq], DX)

    def ag_x_recv(k, zq):
        r = W.at[k, px, zq, y, P1]
        return rc(r, r, sag.at[0, 1, k, zq], sag.at[1, 1, k, zq], DX)

    def ag_y(k, zq, own=False):
        r = W.at[k, p, zq, y, P1]
        return rc(wsl.at[k, P1] if own else r, r, sag.at[0, 2, k, zq], sag.at[1, 2, k, zq], DY_)

    def ag_y_recv(k, zq):
        r = W.at[k, p, zq, yx, P1]
        return rc(r, r, sag.at[0, 2, k, zq], sag.at[1, 2, k, zq], DY_)

    def ag_dy(k, zq):
        r = W.at[k, px, zq, y, PY]
        return rc(r, r, sag.at[0, 3, k, zq], sag.at[1, 3, k, zq], DY_)

    def ag_dy_recv(k, zq):
        r = W.at[k, px, zq, yx, PY]
        return rc(r, r, sag.at[0, 3, k, zq], sag.at[1, 3, k, zq], DY_)

    def ag_dx(k, zq):
        r = W.at[k, p, zq, yx, PX]
        return rc(r, r, sag.at[0, 4, k, zq], sag.at[1, 4, k, zq], DX)

    def ag_dx_recv(k, zq):
        r = W.at[k, px, zq, yx, PX]
        return rc(r, r, sag.at[0, 4, k, zq], sag.at[1, 4, k, zq], DX)

    def aq(k, n):
        dst = W.at[k, px if n == 2 else p, z, y, P2]
        src = dst if n == 2 else wsl.at[k, P2]
        return rc(src, dst, sag.at[0, 5, k, n], sag.at[1, 5, k, n], DX if n == 0 else DY_)

    def aq_recv(k, n):
        r = W.at[k, p if n == 1 else px, z, y if n == 0 else yx, P2]
        return rc(r, r, sag.at[0, 5, k, n], sag.at[1, 5, k, n], DX)

    def aqz(k, o):
        r = W.at[k, :, z, :, P2]
        return rc(r, r, sag.at[0, 6, k, o], sag.at[1, 6, k, z], zdev(zs[o]))

    def aqz_far(k):
        r = W.at[k, :, zs[2], :, P2]
        return rc(r, r, sag.at[0, 6, k, 3], sag.at[1, 6, k, zs[2]], zdev(zs[0]))

    def aqz_recv(k, zq):
        r = W.at[k, :, zq, :, P2]
        return rc(r, r, sag.at[0, 6, k, 0], sag.at[1, 6, k, zq], DX)

    def ag_start(k):
        ag_z(k, 0).start()
        ag_z(k, 1).start()
        when(mid, lambda: ag_z(k, 2).start())

    def ag_events(k):
        def first():
            aq(k, 0).start()
            aq(k, 1).start()
            ag_x(k, z, True).start()
            ag_y(k, z, True).start()

        def relay(o):
            ag_z_recv(k, zs[o]).wait_recv()
            if o == 2:
                when(mid, lambda: ag_far(k).start())
            ag_x(k, zs[o]).start()
            ag_y(k, zs[o]).start()

        def quad():
            aq_recv(k, 0).wait_recv()
            aq(k, 2).start()

        def quad_z():
            aq_recv(k, 1).wait_recv()
            aq_recv(k, 2).wait_recv()
            aqz(k, 0).start()
            aqz(k, 1).start()
            when(mid, lambda: aqz(k, 2).start())

        def from_x(o):
            ag_x_recv(k, zs[o]).wait_recv()
            ag_dy(k, zs[o]).start()

        def from_y(o):
            ag_y_recv(k, zs[o]).wait_recv()
            ag_dx(k, zs[o]).start()

        def far():
            def go():
                aqz_recv(k, zs[2]).wait_recv()
                aqz_far(k).start()

            when(mid, go)

        f = functools.partial
        return dict(
            first=first,
            quad=quad,
            z0=f(relay, 0),
            z1=f(relay, 1),
            z2=f(relay, 2),
            quadz=quad_z,
            x3=f(from_x, 3),
            y3=f(from_y, 3),
            x0=f(from_x, 0),
            y0=f(from_y, 0),
            x1=f(from_x, 1),
            y1=f(from_y, 1),
            x2=f(from_x, 2),
            y2=f(from_y, 2),
            far=far,
        )

    def ag_done(k):
        ag_done_own(k)
        ag_done_other(k)

    def ag_done_other(k):
        for zq in range(NZ):
            ag_dx_recv(k, zq).wait_recv()
            ag_dy_recv(k, zq).wait_recv()

    def ag_done_own(k):
        aqz_recv(k, zs[0]).wait_recv()
        aqz_recv(k, zs[1]).wait_recv()
        when(end, lambda: aqz_recv(k, zs[2]).wait_recv())

    def ag_sent(k):
        for o in (0, 1):
            ag_z(k, o).wait_send()
            aqz(k, o).wait_send()

        def far():
            for cp in (ag_z(k, 2), aqz(k, 2), ag_far(k), aqz_far(k)):
                cp.wait_send()

        when(mid, far)
        for n in range(3):
            aq(k, n).wait_send()
        for zq in range(NZ):
            ag_x(k, zq).wait_send()
            ag_y(k, zq).wait_send()
            ag_dx(k, zq).wait_send()
            ag_dy(k, zq).wait_send()

    def gr(k):
        return W.at[1] if k == 0 else G.at[k - 1]

    NA = R1 - RX
    OB = NZ * NA
    OX = OB + NZ * RX
    OY = OX + NZ * R1
    OL = OY + NZ * R1
    OC = OL + R1
    OQ = NZ * R1
    OLQ = OQ + NZ * 4 * NQ

    def land(k, half, row, n):
        if k == 0:
            return GP.at[half, pl.ds(row, n)]
        return (((MG, LAND1) if k == 1 else (LAND2A, LAND2))[half]).at[pl.ds(row, n)]

    def peers():
        return (DX, DY_, zdev(zs[0]), zdev(zs[1]), zdev(zs[2]))

    def say_free(k):
        for dev in peers():
            pl.semaphore_signal(cred.at[k], 1, device_id=dev, device_id_type=MESH_ID)

    def wait_free(k):
        pl.semaphore_wait(cred.at[k], 5)

    def r1a(k, zq):
        return rc(gr(k).at[px, zq, yx, PY], land(k, 0, zq * NA, NA), srs.at[0, 0, k, zq], srs.at[1, 0, k, zq], DY_)

    def r1b(k, zq):
        return rc(gr(k).at[px, zq, yx, PX], land(k, 0, OB + zq * RX, RX), srs.at[0, 1, k, zq], srs.at[1, 1, k, zq], DX)

    def r2x(k, zq):
        return rc(gr(k).at[px, zq, y, P1], land(k, 0, OX + zq * R1, R1), srs.at[0, 2, k, zq], srs.at[1, 2, k, zq], DX)

    def r2y(k, zq):
        return rc(gr(k).at[p, zq, yx, P1], land(k, 0, OY + zq * R1, R1), srs.at[0, 3, k, zq], srs.at[1, 3, k, zq], DY_)

    def r3(k, o):
        return rc(
            gr(k).at[p, zs[o], y, P1], land(k, 1, z * R1, R1), srs.at[0, 4, k, o], srs.at[1, 4, k, z], zdev(zs[o])
        )

    def r3_recv(k, zq):
        return rc(gr(k).at[p, zq, y, P1], land(k, 1, zq * R1, R1), srs.at[0, 4, k, 0], srs.at[1, 4, k, zq], DX)

    def r3_far(k):
        return rc(gr(k).at[p, zs[2], y, P1], land(k, 0, OL, R1), srs.at[0, 5, k, 0], srs.at[1, 5, k, 0], zdev(zs[0]))

    def side(jj):
        return px if jj == 0 else p

    def rq(k, o, jj, yq):
        j = side(jj)
        n = 2 * j + yq
        return rc(
            gr(k).at[j, zs[o], yq, P2],
            land(k, 1, OQ + (z * 4 + n) * NQ, NQ),
            srs.at[0, 6 + 2 * jj + yq, k, o],
            srs.at[1, 6 + 2 * jj + yq, k, z],
            zdev(zs[o]),
        )

    def rq_recv(k, zq, jj, yq):
        r = land(k, 1, OQ + (zq * 4 + 2 * side(jj) + yq) * NQ, NQ)
        return rc(r, r, srs.at[0, 6 + 2 * jj + yq, k, 0], srs.at[1, 6 + 2 * jj + yq, k, zq], DX)

    def rq_far(k, jj, yq):
        j = side(jj)
        n = 2 * j + yq
        m = 2 * jj + yq
        return rc(
            gr(k).at[j, zs[2], yq, P2], land(k, 1, OLQ + n * NQ, NQ), srs.at[0, 10, k, m], srs.at[1, 10, k, m], zdev(zs[0])
        )

    def rcq(k, n):
        src = gr(k).at[p if n == 2 else px, z, y if n == 1 else yx, P2]
        return rc(src, land(k, 0, OC + n * NQ, NQ), srs.at[0, 11, k, n], srs.at[1, 11, k, n], DX if n == 1 else DY_)

    def add_to(k, idx, *pieces):
        g = gr(k)
        v = g[idx].astype(F32)
        for q in pieces:
            v = v + q[...].astype(F32)
        g[idx] = v.astype(BF)

    def rs_start(k, jj):
        for yq in range(2):
            when(end, lambda yq=yq: rq_far(k, jj, yq).start())
        if jj == 0:
            for o in (2, 0, 1, 3):
                r1a(k, zs[o]).start()
                r1b(k, zs[o]).start()
        for o in (0, 1):
            for yq in range(2):
                rq(k, o, jj, yq).start()

    def rs_a(k, o):
        r1a(k, zs[o]).wait_recv()
        add_to(k, (px, zs[o], y, PY), land(k, 0, zs[o] * NA, NA))
        r2x(k, zs[o]).start()

    def rs_b(k, o):
        r1b(k, zs[o]).wait_recv()
        add_to(k, (p, zs[o], yx, PX), land(k, 0, OB + zs[o] * RX, RX))
        r2y(k, zs[o]).start()

    def rs_pass(k, jj):
        def go():
            for yq in range(2):
                n = 2 * side(jj) + yq
                rq_far(k, jj, yq).wait_recv()
                add_to(k, (side(jj), zs[2], yq, P2), land(k, 1, OLQ + n * NQ, NQ))
                rq(k, 2, jj, yq).start()

        when(mid, go)

    def rs_zsum(k, jj):
        for yq in range(2):

            def take(o, yq=yq):
                rq_recv(k, zs[o], jj, yq).wait_recv()
                add_to(k, (side(jj), z, yq, P2), land(k, 1, OQ + (zs[o] * 4 + 2 * side(jj) + yq) * NQ, NQ))

            take(0)
            take(1)
            when(mid, lambda take=take: take(2))
        rcq(k, 0 if jj == 0 else 2).start()

    def rs_corner(k):
        rcq(k, 0).wait_recv()
        add_to(k, (px, z, y, P2), land(k, 0, OC, NQ))
        rcq(k, 1).start()

    def rs_quad(k, o):
        zq = zs[o]
        r2x(k, zq).wait_recv()
        r2y(k, zq).wait_recv()
        i = (p, zq, y, P1)
        add_to(k, i, land(k, 0, OX + zq * R1, R1), land(k, 0, OY + zq * R1, R1))
        if o < 2:
            r3(k, o).start()
        elif o == 2:
            when(end, lambda: r3_far(k).start())

    def rs_last(k):
        def go():
            r3_far(k).wait_recv()
            add_to(k, (p, zs[2], y, P1), land(k, 0, OL, R1))
            r3(k, 2).start()

        when(mid, go)

    def rs_final(k):
        rcq(k, 1).wait_recv()
        rcq(k, 2).wait_recv()
        g = gr(k)
        v = g[p, z, y, P2].astype(F32)
        for n in (1, 2):
            v = v + land(k, 0, OC + n * NQ, NQ)[...].astype(F32)
        gw_out[k, R1:SR] = v
        gw_out[k, 0:R1] = g[p, z, y, P1].astype(F32)

        def take(o):
            r3_recv(k, zs[o]).wait_recv()
            gw_out[k, 0:R1] += land(k, 1, zs[o] * R1, R1)[...].astype(F32)

        take(0)
        take(1)
        when(mid, lambda: take(2))

    def rs_sent(k):
        for zq in range(NZ):
            r1a(k, zq).wait_send()
            r1b(k, zq).wait_send()
            r2x(k, zq).wait_send()
            r2y(k, zq).wait_send()
        for n in range(3):
            rcq(k, n).wait_send()
        quads = [(jj, yq) for jj in range(2) for yq in range(2)]
        for o in (0, 1):
            r3(k, o).wait_send()
            for jj, yq in quads:
                rq(k, o, jj, yq).wait_send()

        def out():
            r3(k, 2).wait_send()
            for jj, yq in quads:
                rq(k, 2, jj, yq).wait_send()

        def far():
            r3_far(k).wait_send()
            for jj, yq in quads:
                rq_far(k, jj, yq).wait_send()

        when(mid, out)
        when(end, far)

    def rs_events(k):
        f = functools.partial
        return dict(
            start0=f(rs_start, k, 0),
            start1=f(rs_start, k, 1),
            pass0=f(rs_pass, k, 0),
            pass1=f(rs_pass, k, 1),
            a2=f(rs_a, k, 2),
            b2=f(rs_b, k, 2),
            a0=f(rs_a, k, 0),
            b0=f(rs_b, k, 0),
            a1=f(rs_a, k, 1),
            b1=f(rs_b, k, 1),
            a3=f(rs_a, k, 3),
            b3=f(rs_b, k, 3),
            zsum0=f(rs_zsum, k, 0),
            zsum1=f(rs_zsum, k, 1),
            corner=f(rs_corner, k),
            q2=f(rs_quad, k, 2),
            q0=f(rs_quad, k, 0),
            q1=f(rs_quad, k, 1),
            q3=f(rs_quad, k, 3),
            last=f(rs_last, k),
            final=f(rs_final, k),
        )

    A = [ag_events(k) for k in range(3)]
    R = [rs_events(k) for k in range(3)]
    EV = {}
    for k in range(3):
        EV.update({"A%d%s" % (k, n): fn for n, fn in A[k].items()})
        EV.update({"R%d%s" % (k, n): fn for n, fn in R[k].items()})
        EV["A%dgo" % k] = functools.partial(ag_start, k)
    EV["dy"] = lambda: cp_dy().start()
    EV["R1free"] = lambda: wait_free(1)
    EV["R0free"] = lambda: wait_free(0)

    def at(name, i=0):
        for e in PLACE.get((name, i), ()):
            EV[e]()

    def inside(name, i, i0, n, each=1):
        for step in range(n):
            if PLACE.get((name, step * each + i0)):
                pl.when(i == step)(functools.partial(at, name, step * each + i0))

    def loop(n, body, name=None):
        def step(i, carry):
            if name is not None:
                inside(name, i, 0, n)
            body(i)
            return carry

        lax.fori_loop(0, n, step, 0)

    def sm(k):
        return rc(small.at[dpeer(k)], SMR.at[d], ssm.at[0, k], ssm.at[1, d], (dpeer(k), t))

    def sm_recv(k):
        return rc(small.at[0], SMR.at[dpeer(k)], ssm.at[0, k], ssm.at[1, dpeer(k)], DX)

    def ad(k):
        return rc(ADL.at[dpeer(k)], ADP.at[d], sad.at[0, k], sad.at[1, d], (dpeer(k), t))

    def ad_recv(k):
        return rc(ADL.at[0], ADP.at[dpeer(k)], sad.at[0, k], sad.at[1, dpeer(k)], DX)

    def adt(k):
        return rc(ADS, ADT.at[t], sadt.at[0, k], sadt.at[1, t], (d, tpeer(k)))

    def adt_recv(k):
        return rc(ADS, ADT.at[tpeer(k)], sadt.at[0, k], sadt.at[1, tpeer(k)], DX)

    own_x = pltpu.make_async_copy(xin.at[p], X.at[p], sloc.at[0])
    own_x.start()
    own_w = [pltpu.make_async_copy(wsl.at[k], W.at[k, p, z, y], sloc.at[2 + k]) for k in range(3)]
    for cp in own_w:
        cp.start()
    own_dy = pltpu.make_async_copy(dyin.at[p], DYF.at[rows_of(p, c)], sloc.at[1])
    own_dy.start()
    for k in range(1, NDP):
        sm(k).start()
    EV["A0go"]()
    EV["A0first"]()
    cp_x().start()
    SMR[d] = small[d]
    O[...] = jnp.zeros_like(O)
    GQ[...] = jnp.zeros_like(GQ)
    RINV[...] = jnp.zeros_like(RINV)
    ACC[...] = jnp.zeros_like(ACC)
    SLT[...] = jnp.zeros_like(SLT)
    GA2[...] = jnp.zeros_like(GA2)
    GGS[...] = jnp.zeros_like(GGS)
    for cp in own_w:
        cp.wait()
    at("start", 0)
    for k in range(1, NDP):
        sm_recv(k).wait_recv()
    for i in range(NDP):
        VEC[0:1, SR * i : SR * (i + 1)] = SMR[i, 2:3, 0:SR]

    SC = ADT.shape[2] // 2
    feats = SMR[...].reshape(NDP * 8, 128).astype(BF)
    part = mm(feats, adaw[...])
    ADL[...] = part.reshape(NDP, 8, part.shape[1])
    for k in range(1, NDP):
        ad(k).start()
    ADP[d] = ADL[d]

    def ada_sum():
        for k in range(1, NDP):
            ad_recv(k).wait_recv()
        tot = ADP[0]
        for i in range(1, NDP):
            tot = tot + ADP[i]
        ADS[...] = tot
        for k in range(1, 4):
            adt(k).start()
        ADT[t] = tot

    def ada_vec():
        for k in range(1, 4):
            adt_recv(k).wait_recv()
        for tt in range(4):
            VEC[1:2, SC * tt : SC * (tt + 1)] = 1.0 + ADT[tt, pl.ds(p, 1), 0:SC]
            VEC[2:3, SC * tt : SC * (tt + 1)] = ADT[tt, pl.ds(p, 1), SC : 2 * SC]

    RT = 64

    def ln1(j):
        def body(i):
            r = pl.ds(pl.multiple_of(i * RT, RT), RT)
            mean, cen, inv = row_stats(X[j, r, :].astype(F32))
            AIN[pl.ds(pl.multiple_of((2 * j + c) * PC + i * RT, RT), RT), :] = (
                cen * inv * VEC[0:1, :]
            ).astype(BF)

        loop(PC // RT, body)
        cp_full(AIN, 0, j).start()

    at("ln1", 0)
    own_x.wait()
    ln1(p)
    at("ln1", 1)
    cp_x_recv().wait_recv()
    ln1(px)
    at("own", 0)
    for j in range(2):
        cp_full_recv(AIN, 0, j).wait_recv()
    ag_done_own(0)

    def wfull(k, j, cols=None):
        v = W[k, j] if cols is None else W[k, j, :, :, :, cols]
        return v.reshape(D, v.shape[-1])

    HT = T // 2

    def qkv_side(j, name):
        def body(h):
            r = pl.ds(pl.multiple_of(h * HT, HT), HT)
            res = mm(AIN[r, :], wfull(0, j, pl.ds(0, 640)))
            cos, sin = cos_t[r, :], sin_t[r, :]
            rot = []
            for n in range(3):
                x = res[:, 128 * n : 128 * n + 128]
                rot.append(x * cos + swap_halves(x) * sin)
            low = lanes((HT, 128)) < 64
            k1, k2 = pltpu.roll(rot[1], 64, 1), pltpu.roll(rot[2], 64, 1)
            Q[j, r, 0:128] = (rot[0] * 0.125).astype(BF)
            Q[j, r, 128:256] = (rot[1] * 0.125).astype(BF)
            K[j, r, 0:128] = jnp.where(low, k1, k2).astype(BF)
            K[j, r, 128:256] = k2.astype(BF)
            V[j, r, :] = res[:, 384:640].astype(BF)

        loop(2, body, name)

    pfx = pref[p]
    C0, C1 = 512, 768
    GROUPS = ((0, 512), (512, 256), (768, 256))

    def head_lanes(shape, hh):
        return lax.div(lanes(shape), HD) == hh

    def attend_side(j, name):
        def body(hh):
            g = j * 3 + hh
            for n, (r0, nr) in enumerate(GROUPS):
                inside(name, hh, n, 3, 3)
                q = jnp.where(head_lanes((nr, 256), hh), Q[j, r0 : r0 + nr, :], jnp.zeros((), BF))
                spans = [(0, C0), (C0, C1), (C1, T)][: n + 1]
                sc = []
                for n2, (k0, k1) in enumerate(spans):
                    s = mm_nt(q, K[j, k0:k1, :])
                    if n2 == n:
                        row = lax.broadcasted_iota(jnp.int32, s.shape, 0) + r0
                        col = lax.broadcasted_iota(jnp.int32, s.shape, 1) + k0
                        ok = col <= row
                        if n == 0:
                            ok = ok | (col < pfx)
                        s = jnp.where(ok, s, NEG)
                    sc.append(s)
                m = jnp.max(sc[0], axis=1, keepdims=True)
                for s in sc[1:]:
                    m = jnp.maximum(m, jnp.max(s, axis=1, keepdims=True))
                acc, tot = None, None
                for n2, (k0, k1) in enumerate(spans):
                    e = jnp.exp(sc[n2] - m)
                    l = jnp.sum(e, axis=1, keepdims=True)
                    tot = l if tot is None else tot + l
                    eb = e.astype(BF)
                    if n2 == 0:
                        EA[g, r0 : r0 + nr, :] = eb
                    elif n2 == 1:
                        EB[g, r0 - C0 : r0 - C0 + nr, :] = eb
                    else:
                        EC[g] = eb
                    o = mm(eb, V[j, k0:k1, :])
                    acc = o if acc is None else acc + o
                rinv = 1.0 / tot
                old = RINV[r0 : r0 + nr, :]
                RINV[r0 : r0 + nr, :] = jnp.where(lanes((nr, 128)) == g, rinv, old)
                o = (acc * rinv).astype(BF)
                O[j, r0 : r0 + nr, :] = jnp.where(head_lanes((nr, 256), hh), o, O[j, r0 : r0 + nr, :])

        loop(3, body)

    qkv_side(p, "qkv0")
    attend_side(p, "att0")
    at("other", 0)
    ag_done_other(0)
    ada_sum()
    qkv_side(px, "qkv1")
    attend_side(px, "att1")

    low = lanes((D, 128)) < 64
    for j in range(2):
        w = wfull(0, j, pl.ds(512, 256)).astype(F32)
        t4, t5 = pltpu.roll(w[:, 0:128], 64, 1), pltpu.roll(w[:, 128:256], 64, 1)
        MT[j, :, 0:128] = jnp.where(low, t4, t5).astype(BF)
        MT[j, :, 128:256] = t5.astype(BF)

    def two(ref, j, cc):
        return jnp.concatenate([ref[j, rows_of(0, cc), :], ref[j, rows_of(1, cc), :]], axis=0)

    def split_sum(n, body, nt, name):
        width = D // nt

        def send(i):
            cols = pl.ds(pl.multiple_of(i * width, width), width)
            v = body(cx, i)
            PS[PSET[n], 0, :, cols] = v[0:PC].astype(BF)
            PS[PSET[n], 1, :, cols] = v[PC:].astype(BF)

        at(name, 0)
        loop(nt, send)
        for j in range(2):
            cp_part(n, j).start()
        at(name, 1)

        def own(i):
            cols = pl.ds(pl.multiple_of(i * width, width), width)
            v = body(c, i)
            OWN[0, :, cols] = v[0:PC]
            OWN[1, :, cols] = v[PC:]

        loop(nt, own)

    def mix_cols(cc, i):
        cols = pl.ds(pl.multiple_of(i * 256, 256), 256)
        return mm_nt(two(O, 0, cc), MT[0, cols, :]) + mm_nt(two(O, 1, cc), MT[1, cols, :])

    split_sum(0, mix_cols, D // 256, "mix")
    ada_vec()

    def ln2(j):
        cp_part(0, j).wait_recv()

        def body(i):
            r = pl.ds(pl.multiple_of(i * RT, RT), RT)
            res = X[j, r, :].astype(F32) + OWN[j, r, :] + PR[PSET[0], j, r, :].astype(F32)
            RES[j, r, :] = res
            mean, cen, inv = row_stats(res)
            ST[j, r, :] = jnp.where(lanes((RT, 128)) == 0, mean, inv)
            MG[pl.ds(pl.multiple_of((2 * j + c) * PC + i * RT, RT), RT), :] = (
                cen * inv * VEC[1:2, :] + VEC[2:3, :]
            ).astype(BF)

        loop(PC // RT, body)
        cp_full(MG, 1, j).start()

    at("ln2", 0)
    ln2(0)
    at("ln2", 1)
    ln2(1)
    at("all1", 0)
    ag_done(1)
    for j in range(2):
        cp_full_recv(MG, 1, j).wait_recv()

    CA, CB = 0.7978845608028654, 0.044715

    def tile3(i):
        j, rest = lax.div(i, 6), lax.rem(i, 6)
        h, n = lax.div(rest, 3), lax.rem(rest, 3)
        return j, pl.ds(pl.multiple_of(h * HT, HT), HT), pl.ds(pl.multiple_of(n * 256, 256), 256)

    def up_body(i):
        j, r, cols = tile3(i)
        v = mm(MG[r, :], wfull(1, j, cols))
        v2 = v * v
        th = jnp.tanh(CA * v * (1.0 + CB * v2))
        half = 0.5 + 0.5 * th
        HID[j, r, cols] = (v * half).astype(BF)
        slope = (0.5 * CA) * (1.0 + (3.0 * CB) * v2)
        GP[j, r, cols] = (half + v * (1.0 - th * th) * slope).astype(BF)

    loop(12, up_body, "up")

    at("dyw", 0)
    own_dy.wait()
    cp_dy_recv().wait_recv()
    for j in range(2):
        cp_full(DYF, 2, j).start()
    for j in range(2):
        cp_full_recv(DYF, 2, j).wait_recv()

    def wgrad(k, lhs, rhs):
        def body(i):
            j, n = lax.div(i, 3), lax.rem(i, 3)
            cols = pl.ds(pl.multiple_of(n * 256, 256), 256)
            v = mm_tn(lhs[...], rhs[j, :, cols]).astype(BF)
            gr(k)[j, :, :, :, cols] = v.reshape(NZ, 2, SR, 256)

        return body

    loop(6, wgrad(2, DYF, HID), "wg2")
    at("all2", 0)
    ag_done(2)

    def ff_split(n, k, src, name):
        nt = 2
        per = NZ // nt
        width = D // nt

        def body(cc, i):
            w0 = W[k, 0, pl.ds(i * per, per)].reshape(width, W.shape[-1])
            w1 = W[k, 1, pl.ds(i * per, per)].reshape(width, W.shape[-1])
            return mm_nt(two(src, 0, cc), w0) + mm_nt(two(src, 1, cc), w1)

        split_sum(n, body, nt, name)

    def ghid_body(i):
        j, r, cols = tile3(i)
        v = mm(DYF[r, :], wfull(2, j, cols))
        GP[j, r, cols] = (GP[j, r, cols].astype(F32) * v).astype(BF)

    loop(12, ghid_body, "gh")
    ff_split(2, 1, GP, "gu")

    def fold(v):
        return jnp.sum(v.reshape(RT // 8, 8, D), axis=0)

    def ln2_back(j):
        cp_part(2, j).wait_recv()

        def body(i):
            r = pl.ds(pl.multiple_of(i * RT, RT), RT)
            rows = pl.ds(pl.multiple_of((2 * j + c) * PC + i * RT, RT), RT)
            gu = OWN[j, r, :] + PR[PSET[2], j, r, :].astype(F32)
            st = ST[j, r, :]
            mean, inv = st[:, 0:1], st[:, 1:2]
            nrm = (RES[j, r, :] - mean) * inv
            ACC[0] += fold(gu * nrm)
            ACC[1] += fold(gu)
            g = gu * VEC[1:2, :]
            mg = jnp.mean(g, axis=-1, keepdims=True)
            mc = jnp.mean(g * nrm, axis=-1, keepdims=True)
            GA[rows, :] = (DYF[rows, :].astype(F32) + inv * (g - mg - nrm * mc)).astype(BF)

        loop(PC // RT, body)
        cp_full(GA, 3, j).start()

    GA = DYF
    for j in range(2):
        cp_full(DYF, 2, j).wait_send()
    at("l2b", 0)
    ln2_back(0)
    at("l2b", 1)
    ln2_back(1)
    for j in range(2):
        cp_full(MG, 1, j).wait_send()
    loop(6, wgrad(1, MG, GP), "wg1")
    say_free(1)
    say_free(0)

    def rt(k):
        return rc(SLT.at[tpeer(k)], RTT.at[t], srt.at[0, k], srt.at[1, t], (d, tpeer(k)))

    def rt_recv(k):
        return rc(SLT.at[0], RTT.at[tpeer(k)], srt.at[0, k], srt.at[1, tpeer(k)], DX)

    def gal(k):
        return rc(GA2, GAL.at[d], sgal.at[0, k], sgal.at[1, d], (dpeer(k), t))

    def gal_recv(k):
        return rc(GA2, GAL.at[dpeer(k)], sgal.at[0, k], sgal.at[1, dpeer(k)], DX)

    for n in range(2):
        row = jnp.sum(ACC[n], axis=0, keepdims=True)
        for tt in range(4):
            SLT[tt, n : n + 1, 0:SC] = row[:, SC * tt : SC * (tt + 1)]
    for k in range(1, 4):
        rt(k).start()
    RTT[t] = SLT[t]
    for j in range(2):
        cp_full_recv(GA, 3, j).wait_recv()
    ag_sent(1)

    def back_side(jj, name):
        j = px if jj == 0 else p

        def gmix(h):
            r = pl.ds(pl.multiple_of(h * HT, HT), HT)
            do = mm(GA[r, :], MT[j]).astype(BF).astype(F32)
            o = O[j, r, :].astype(F32)
            ri = RINV[r, :]
            dl = jnp.zeros((HT, 128), F32)
            for hh in range(3):
                g3 = j * 3 + hh
                rh = jnp.sum(jnp.where(lanes((HT, 128)) == g3, ri, 0.0), axis=1, keepdims=True)
                dm = jnp.where(head_lanes((HT, 256), hh), do * rh, 0.0)
                M3[hh, r, :] = dm.astype(BF)
                dl = jnp.where(lanes((HT, 128)) == hh, jnp.sum(dm * o, axis=1, keepdims=True), dl)
            DEL[r, :] = dl

        at(name, 0)
        loop(2, gmix)
        at(name, 1)

        def e_dot(k0, nk):
            acc = None
            for hh in range(3):
                g = j * 3 + hh
                if k0 < C0:
                    v = mm_tn(EA[g, :, k0 : k0 + nk], M3[hh])
                elif k0 < C1:
                    v = mm_tn(EB[g], M3[hh, C0:T, :])
                else:
                    v = mm_tn(EC[g], M3[hh, C1:T, :])
                acc = v if acc is None else acc + v
            return acc

        KB = ((0, 256), (256, 256), (512, 256), (768, 256))
        for k0, nk in KB:
            GQ[j, k0 : k0 + nk, 384:640] = e_dot(k0, nk).astype(BF)
        at(name, 2)

        def ds_body(hh):
            inside(name, hh, 3, 3)
            g = j * 3 + hh
            for n, (r0, nr) in enumerate(GROUPS):
                dm = M3[hh, r0 : r0 + nr, :]
                dl = jnp.sum(
                    jnp.where(lanes((nr, 128)) == hh, DEL[r0 : r0 + nr, :], 0.0), axis=1, keepdims=True
                )
                spans = [(0, C0), (C0, C1), (C1, T)][: n + 1]
                for n2, (k0, k1) in enumerate(spans):
                    dp = mm_nt(dm, V[j, k0:k1, :]) - dl
                    if n2 == 0:
                        EA[g, r0 : r0 + nr, :] = (EA[g, r0 : r0 + nr, :].astype(F32) * dp).astype(BF)
                    elif n2 == 1:
                        e0 = r0 - C0
                        EB[g, e0 : e0 + nr, :] = (EB[g, e0 : e0 + nr, :].astype(F32) * dp).astype(BF)
                    else:
                        EC[g] = (EC[g].astype(F32) * dp).astype(BF)

        loop(3, ds_body)
        at(name, 6)

        for n, (r0, nr) in enumerate(GROUPS):
            acc = None
            for hh in range(3):
                g = j * 3 + hh
                for n2, (k0, k1) in enumerate([(0, C0), (C0, C1), (C1, T)][: n + 1]):
                    kk = K[j, k0:k1, :]
                    km = jnp.where(head_lanes(kk.shape, hh), kk, jnp.zeros((), BF))
                    if n2 == 0:
                        s = EA[g, r0 : r0 + nr, :]
                    elif n2 == 1:
                        s = EB[g, r0 - C0 : r0 - C0 + nr, :]
                    else:
                        s = EC[g]
                    v = mm(s, km)
                    acc = v if acc is None else acc + v
            acc = acc * 0.125
            cos, sin = cos_t[r0 : r0 + nr, :], sin_t[r0 : r0 + nr, :]
            for n2 in range(2):
                x = acc[:, 128 * n2 : 128 * n2 + 128]
                GQ[j, r0 : r0 + nr, 128 * n2 : 128 * n2 + 128] = (x * cos - swap_halves(x) * sin).astype(BF)
        at(name, 7)
        for hh in range(3):
            qq = Q[j]
            M3[hh] = jnp.where(head_lanes(qq.shape, hh), qq, jnp.zeros((), BF))
        for k0, nk in KB:
            v = e_dot(k0, nk)
            cos, sin = cos_t[k0 : k0 + nk, :], sin_t[k0 : k0 + nk, :]
            un = []
            for n2 in range(2):
                x = v[:, 128 * n2 : 128 * n2 + 128]
                un.append(pltpu.roll(x * cos - swap_halves(x) * sin, 64, 1))
            lowk = lanes((nk, 128)) < 64
            old = GQ[j, k0 : k0 + nk, 128:256].astype(F32)
            GQ[j, k0 : k0 + nk, 128:256] = jnp.where(lowk, old, un[0]).astype(BF)
            GQ[j, k0 : k0 + nk, 256:384] = jnp.where(lowk, un[0], un[1]).astype(BF)
        at(name, 8)

        g0 = gr(0)
        for n in range(2):
            v = mm_tn(AIN[...], GQ[j, :, 256 * n : 256 * n + 256]).astype(BF)
            g0[j, :, :, :, 256 * n : 256 * n + 256] = v.reshape(NZ, 2, SR, 256)
        gv = mm_tn(AIN[...], GQ[j, :, 512:640])
        gm = mm_tn(GA[...], O[j])
        m0, m1 = pltpu.roll(gm[:, 0:128], 64, 1), pltpu.roll(gm[:, 128:256], 64, 1)
        lowd = lanes((D, 128)) < 64
        g0[j, :, :, :, 512:640] = jnp.where(lowd, gv, m0).astype(BF).reshape(NZ, 2, SR, 128)
        g0[j, :, :, :, 640:768] = jnp.where(lowd, m0, m1).astype(BF).reshape(NZ, 2, SR, 128)

    back_side(0, "s0")

    for k in range(1, 4):
        rt_recv(k).wait_recv()
    for s in range(2):
        v = RTT[2 * s] + RTT[2 * s + 1]
        for n in range(2):
            GA2[n, s : s + 1, :] = v[n : n + 1, :]
    for k in range(1, NDP):
        gal(k).start()
    GAL[d] = GA2[...]

    back_side(1, "s1")

    def in_cols(cc, i):
        per = NZ // 2
        acc = None
        for j in range(2):
            w = W[0, j, pl.ds(i * per, per), :, :, pl.ds(0, 640)].reshape(D // 2, 640)
            v = mm_nt(two(GQ, j, cc), w)
            acc = v if acc is None else acc + v
        return acc

    for j in range(2):
        cp_part(0, j).wait_send()
    split_sum(3, in_cols, 2, "in")

    def ln1_back(jj):
        j = px if jj == 0 else p
        cp_part(3, j).wait_recv()

        def body(i):
            r = pl.ds(pl.multiple_of(i * RT, RT), RT)
            rows = pl.ds(pl.multiple_of((2 * j + c) * PC + i * RT, RT), RT)
            gi = OWN[j, r, :] + PR[PSET[3], j, r, :].astype(F32)
            mean, cen, inv = row_stats(X[j, r, :].astype(F32))
            nrm = cen * inv
            ACC[2] += fold(gi * nrm)
            g = gi * VEC[0:1, :]
            mg = jnp.mean(g, axis=-1, keepdims=True)
            mc = jnp.mean(g * nrm, axis=-1, keepdims=True)
            out = (GA[rows, :].astype(F32) + inv * (g - mg - nrm * mc)).astype(BF)
            if jj == 0:
                IGS[r, :] = out
            else:
                ig_out[p, r, :] = out

        loop(PC // RT, body)
        if jj == 0:
            cp_ig().start()

    at("l1b", 0)
    ln1_back(0)
    at("l1b", 1)
    ln1_back(1)

    def gt(k):
        return rc(GGT.at[t], GGT.at[t], sgt.at[0, k], sgt.at[1, t], (d, tpeer(k)))

    def gt_recv(k):
        return rc(GGT.at[t], GGT.at[tpeer(k)], sgt.at[0, k], sgt.at[1, tpeer(k)], DX)

    def grd(k):
        return rc(GGS.at[dpeer(k)], GGR.at[d], sgr.at[0, k], sgr.at[1, d], (dpeer(k), t))

    def grd_recv(k):
        return rc(GGS.at[0], GGR.at[dpeer(k)], sgr.at[0, k], sgr.at[1, dpeer(k)], DX)

    GGT[t] = ACC[2]
    for k in range(1, 4):
        gt(k).start()

    for j in range(2):
        cp_part(2, j).wait_send()
    ff_split(1, 2, HID, "down")

    for k in range(1, 4):
        gt_recv(k).wait_recv()
    row = jnp.sum(GGT[0] + GGT[1] + GGT[2] + GGT[3], axis=0, keepdims=True)
    for i in range(NDP):
        GGS[i, 0:1, 0:SR] = row[:, SR * i : SR * (i + 1)]
    for k in range(1, NDP):
        grd(k).start()
    GGR[d] = GGS[d]

    def layer_out(jj):
        j = px if jj == 0 else p
        cp_part(1, j).wait_recv()

        def body(i):
            r = pl.ds(pl.multiple_of(i * RT, RT), RT)
            v = (RES[j, r, :] + OWN[j, r, :] + PR[PSET[1], j, r, :].astype(F32)).astype(BF)
            if jj == 0:
                LOS[r, :] = v
            else:
                lo_out[p, r, :] = v

        loop(PC // RT, body)
        if jj == 0:
            cp_lo().start()

    at("lo", 0)
    layer_out(0)
    at("lo", 1)
    layer_out(1)

    for k in range(1, NDP):
        gal_recv(k).wait_recv()
    feat = SMR[...].reshape(NDP * 8, 128)
    for n in range(2):
        v = lax.dot_general(
            feat,
            GAL[:, n].reshape(NDP * 8, 256),
            (((0,), (0,)), ((), ())),
            preferred_element_type=F32,
            precision=lax.Precision.HIGHEST,
        )
        ga_out[n] = v[0:SR, 0:SC]
    at("end", 0)
    for k in range(1, NDP):
        grd_recv(k).wait_recv()
    tot = GGR[0]
    for i in range(1, NDP):
        tot = tot + GGR[i]
    gg_out[...] = tot

    cp_x().wait_send()
    cp_dy().wait_send()
    cp_lo().wait_send()
    cp_lo_recv().wait_recv()
    cp_ig().wait_send()
    cp_ig_recv().wait_recv()
    for j in range(2):
        cp_full(AIN, 0, j).wait_send()
        cp_full(GA, 3, j).wait_send()
        cp_part(1, j).wait_send()
        cp_part(3, j).wait_send()
    ag_sent(0)
    ag_sent(2)
    for k in range(3):
        rs_sent(k)
    for k in range(1, NDP):
        sm(k).wait_send()
        ad(k).wait_send()
        gal(k).wait_send()
        grd(k).wait_send()
    for k in range(1, 4):
        adt(k).wait_send()
        rt(k).wait_send()
        gt(k).wait_send()


def fused_local(layer_in, prefix_len, time_step, norm_gain, qkv_weight, mix_weight, ada_weight, up_weight, down_weight, out_grad):
    ndp = lax.axis_size("dp")
    _, pc, width = layer_in.shape
    length = pc * 4
    sr = width // ndp
    nz = ndp // 2
    temb = time_features(time_step, width).astype(jnp.bfloat16).astype(jnp.float32)
    feat = jnp.moveaxis(temb.reshape(2, ndp, sr), 0, 1)
    gain = jnp.broadcast_to(norm_gain.astype(jnp.float32)[None, None], (ndp, 1, sr))
    small = jnp.concatenate([feat, gain], axis=1)
    small = jnp.pad(small, ((0, 0), (0, 5), (0, 128 - sr)))
    wsl = jnp.stack(
        [
            jnp.concatenate([qkv_weight.reshape(sr, -1), mix_weight.T], axis=1),
            up_weight,
            down_weight.T,
        ]
    )
    sc = ada_weight.shape[2]
    adaw = jnp.pad(ada_weight.reshape(sr, 2 * sc), ((0, 128 - sr), (0, 0)))
    cosn, sinn = rope_tables(length)
    dims = (ndp, nz, sr, width, length, pc)
    bf, f32 = jnp.bfloat16, jnp.float32
    vm = pltpu.VMEM
    dma = pltpu.SemaphoreType.DMA
    scratch = [
        vm((3, 2, nz, 2, sr, width), bf),
        vm((2, pc, width), bf),
        vm((length, width), bf),
        vm((length, width), bf),
        vm((length, width), bf),
        vm((2, length, 256), bf),
        vm((2, length, 256), bf),
        vm((2, length, 256), bf),
        vm((6, length, 512), bf),
        vm((6, 512, 256), bf),
        vm((6, 256, 256), bf),
        vm((2, length, 256), bf),
        vm((length, 128), f32),
        vm((2, width, 256), bf),
        vm((2, pc, width), f32),
        vm((2, pc, 128), f32),
        vm((2, pc, width), f32),
        vm((2, 2, pc, width), bf),
        vm((2, 2, pc, width), bf),
        vm((2, length, width), bf),
        vm((2, length, width), bf),
        vm((3, length, 256), bf),
        vm((length, 128), f32),
        vm((2, length, 640), bf),
        vm((2, 2, nz, 2, sr, width), bf),
        vm((length, width), bf),
        vm((length * 3 // 4, width), bf),
        vm((length * 3 // 4, width), bf),
        vm((pc, width), bf),
        vm((pc, width), bf),
        vm((ndp, 8, 128), f32),
        vm((ndp, 8, 2 * sc), f32),
        vm((ndp, 8, 2 * sc), f32),
        vm((8, 2 * sc), f32),
        vm((4, 8, 2 * sc), f32),
        vm((8, width), f32),
        vm((3, 8, width), f32),
        vm((4, 8, 256), f32),
        vm((4, 8, 256), f32),
        vm((2, 8, 256), f32),
        vm((ndp, 2, 8, 256), f32),
        vm((4, 8, width), f32),
        vm((ndp, 8, 128), f32),
        vm((ndp, 8, 128), f32),
        dma((4, 2)),
        dma((2, 7, 3, nz)),
        dma((2, 12, 3, nz)),
        pltpu.SemaphoreType.REGULAR((2,)),
        dma((2, 8, 2)),
        dma((2, ndp)),
        dma((2, ndp)),
        dma((2, 4)),
        dma((2, 4)),
        dma((2, ndp)),
        dma((2, 4)),
        dma((2, ndp)),
        dma((5,)),
    ]
    vspec = pl.BlockSpec(memory_space=pltpu.VMEM)
    lo, ig, gw, ga, gg = pl.pallas_call(
        functools.partial(layer_kernel, dims),
        out_shape=(
            jax.ShapeDtypeStruct((2, pc, width), bf),
            jax.ShapeDtypeStruct((2, pc, width), bf),
            jax.ShapeDtypeStruct((3, sr, width), f32),
            jax.ShapeDtypeStruct((2, sr, sc), f32),
            jax.ShapeDtypeStruct((8, 128), f32),
        ),
        in_specs=[pl.BlockSpec(memory_space=pltpu.SMEM), vspec] + [pl.BlockSpec(memory_space=pl.ANY)] * 2 + [vspec] * 4,
        out_specs=(vspec,) * 5,
        scratch_shapes=scratch,
        compiler_params=pltpu.CompilerParams(
            collective_id=0, has_side_effects=True, vmem_limit_bytes=67043328
        ),
        name="layer_step",
    )(prefix_len, small, layer_in, out_grad, wsl, adaw, cosn, sinn)
    qm = 3 * sc
    return (
        lo,
        ig,
        gg[0, :sr],
        gw[0, :, :qm].reshape(sr, 3, sc),
        gw[0, :, qm:].T,
        jnp.moveaxis(ga, 0, 1),
        gw[1],
        gw[2].T,
    )


def rope_tables(length):
    half = HD // 2
    freq = np.exp(np.arange(half, dtype=np.float32) * np.float32(-math.log(10000.0) / half)).astype(np.float32)
    ang = np.arange(length, dtype=np.float32)[:, None] * freq[None, :]
    cos, sin = np.cos(ang).astype(np.float32), np.sin(ang).astype(np.float32)
    return np.concatenate([cos] * 4, axis=1), np.concatenate([-sin, sin] * 2, axis=1)


PLACE = {
    ("start", 0): ("A0quad", "A0quadz", "A0z0", "A0z1", "A0y3", "A1first", "A2first", "A1go",),
    ("ln1", 0): ("A0z2", "A0x3", "A0far", "A1quad", "A0y2",),
    ("ln1", 1): ("A0y0", "A0x1", "A1x3",),
    ("own", 0): ("A1quadz", "A0y1",),
    ("qkv0", 1): ("A1z0",),
    ("att0", 0): ("A0x0",),
    ("att0", 1): ("A1z1", "dy", "A2go",),
    ("att0", 3): ("A0x2",),
    ("att0", 6): ("A1z2",),
    ("att0", 7): ("A1y0",),
    ("att0", 8): ("A1x1",),
    ("qkv1", 1): ("A2quad",),
    ("att1", 0): ("A2x3",),
    ("att1", 2): ("A1far",),
    ("att1", 4): ("A1x0", "A1y1",),
    ("att1", 5): ("A1y2",),
    ("att1", 6): ("A1y3",),
    ("att1", 7): ("A2z0", "A2quadz", "A2y3",),
    ("mix", 1): ("A1x2",),
    ("ln2", 1): ("A2z1",),
    ("all1", 0): ("A2x0",),
    ("up", 5): ("A2z2",),
    ("up", 6): ("A2x1",),
    ("up", 7): ("A2y1",),
    ("dyw", 0): ("A2y0",),
    ("wg2", 0): ("A2x2",),
    ("wg2", 2): ("A2y2", "A2far",),
    ("gh", 1): ("R2start0",),
    ("gh", 10): ("R2start1",),
    ("gh", 11): ("R2a2", "R2b2", "R2b3",),
    ("gu", 0): ("R2b1", "R2b0",),
    ("wg1", 0): ("R2a0",),
    ("wg1", 1): ("R2q2", "R2pass0",),
    ("wg1", 2): ("R2a1", "R2a3",),
    ("s0", 0): ("R2pass1", "R2zsum0",),
    ("s0", 3): ("R2q1", "R2q0",),
    ("s0", 5): ("R2zsum1",),
    ("s0", 6): ("R1free",),
    ("s0", 7): ("R2q3", "R1start1", "R1start0", "R2corner",),
    ("s1", 0): ("R1b2", "R0free", "R0start0",),
    ("s1", 1): ("R2last",),
    ("s1", 2): ("R1b0",),
    ("s1", 4): ("R1a0",),
    ("s1", 6): ("R1b3",),
    ("s1", 7): ("R1a2", "R1a1",),
    ("in", 0): ("R1pass1", "R1b1",),
    ("in", 1): ("R1a3",),
    ("l1b", 0): ("R2final", "R0pass0", "R0a2",),
    ("l1b", 1): ("R0a0",),
    ("down", 0): ("R0a3", "R0start1", "R0b3",),
    ("down", 1): ("R1q0", "R0a1",),
    ("lo", 0): ("R0b2", "R0b1",),
    ("lo", 1): ("R0b0",),
    ("end", 0): ("R1q2", "R1pass0", "R0pass1", "R1last", "R0zsum0", "R1q1", "R1zsum1", "R1q3", "R0zsum1", "R0q2", "R0q0", "R0last", "R1zsum0", "R1corner", "R0q1", "R0corner", "R1final", "R0q3", "R0final",),
}


def one_kernel(mesh, shapes=None):
    return mesh.shape["tensor"] == 4 and mesh.shape["dp"] == 8


def solution(mesh):
    return jax.shard_map(
        fused_local if one_kernel(mesh) else local,
        mesh=mesh,
        in_specs=(
            P("dp", "tensor", None),
            P("dp"),
            P("dp"),
            P("dp"),
            P("dp", None, "tensor"),
            P("tensor", "dp"),
            P("dp", None, "tensor"),
            P("dp", "tensor"),
            P("tensor", "dp"),
            P("dp", "tensor", None),
        ),
        out_specs=(
            P("dp", "tensor", None),
            P("dp", "tensor", None),
            P("dp"),
            P("dp", None, "tensor"),
            P("tensor", "dp"),
            P("dp", None, "tensor"),
            P("dp", "tensor"),
            P("tensor", "dp"),
        ),
        check_vma=False,
    )
```
